32 devices in a mesh: tok: 16 (over z, x, core), head: 2 (over y).
Axes of the slice: x: 2, y: 2, z: 4, core: 2. Of those that a mesh axis runs over, the one named last changes fastest.
Arguments:
- hidden: bfloat16 [4096, 1536], P(('tok', 'head')), may hold values from -6 to 6
- attn_gain: float32 [1536], replicated, may hold values from 0.1 to 1.9
- w_qkv: bfloat16 [1536, 2560], P(None, 'head'), may hold values from -11 to 11
- kv_cache: bfloat16 [4096, 1024], P('tok', 'head'), may hold values from -38 to 38
- page_table: int32 [256], replicated, may hold values from 0 to 255, each once
- lengths: int32 [64], replicated, may hold values from 1 to 256, as said below
- request_group: int32 [64], replicated, may hold values from 0 to 1
- key_mask: int32 [4096], replicated, may hold values 0 or 1
- o_weight: bfloat16 [1536, 1536], replicated, may hold values from -3.5 to 3.5
- moe_gain: float32 [1536], replicated, may hold values from 0.1 to 1.9
- router: bfloat16 [1536, 16], replicated, may hold values from -151 to 151
- routes: int32 [4096, 8], P(('tok', 'head')), may hold values from 0 to 15, all different within a row; in each aligned block of 128 rows (0 to 127, 128 to 255, ...) at most 96 rows name the same one
- w_gate_up: bfloat16 [16, 1536, 1024], P('tok'), may hold values from -0.21875 to 0.21875
- w_down: bfloat16 [16, 512, 1536], P('tok'), may hold values from -0.5 to 0.5
Outputs:
- attn_branch: bfloat16 [4096, 1536], P(('tok', 'head'))
- layer_out: bfloat16 [4096, 1536], P(('tok', 'head'))
The draws below stay inside these ranges and needn't reach their ends.
Inputs may be any that keep to these rules, and one draw needn't show every extreme that they name: `page_table`: each page appears once. The lengths sum to 4096; the largest is exactly 256. `routes`: the 8 experts of a token differ. Among the rows of one device no expert is named more than 96 times, and in every draw some expert is named exactly 96 times among some device's rows.
All inputs are finite; a program needn't handle non-finite values.
Results may differ from the reference program's by a relative error of at most 0.015.
Values may be sent and summed in bfloat16 or wider, within the bound.
No kernel may reach another device: no remote copies, remote signals or barrier semaphores. Data moves between devices by JAX's collectives and lax.ppermute only.
A program may use at most 192 MiB of HBM per device.

```python
import math
import jax
import jax.numpy as jnp
import numpy as np
from jax import lax

D = 1536
HEADS = 24
KVH = 8
HD = 64
FFE = 512
TOPK = 8
EXPERTS = 16
TOK_DEV = 128
ROW_TOKENS = 256
TOKENS = 4096
PREFIX = 2048
GROUPS = 2
PAGE = 16
POOL_PAGES = 256
REQS = 64
CAP = 96
N_TOK = 16


ROUTER_SCALE = 0.25


def draw_w_qkv(key, part):
    width = (HEADS // KVH + 2) * HD
    entries = jax.random.truncated_normal(jax.random.fold_in(key, 1), -6.0, 6.0, (D, KVH * width), jnp.float32) / D ** 0.5
    return entries.astype(jnp.bfloat16)


def draw_kv_cache(key, part):
    row_count = GROUPS * PREFIX
    col_count = KVH * 2 * HD
    entries = jax.random.truncated_normal(jax.random.fold_in(key, 2), -6.0, 6.0, (row_count, col_count), jnp.float32)
    return entries.astype(jnp.bfloat16)


def draw_router(key, part):
    entries = ROUTER_SCALE * jax.random.truncated_normal(jax.random.fold_in(key, 3), -6.0, 6.0, (D, EXPERTS), jnp.float32) / D ** 0.5
    return entries.astype(jnp.bfloat16)


def draw_lengths(key, part):
    half_row = ROW_TOKENS // 2
    middle_blocks = N_TOK - 2
    lead_cut = jax.random.randint(jax.random.fold_in(key, 11), (middle_blocks,), 1, max(2, half_row // 4 + 1), jnp.int32)
    reach_past = jax.random.randint(jax.random.fold_in(key, 12), (middle_blocks,), half_row // 2, 3 * half_row // 4 + 1, jnp.int32)
    crossing = half_row - lead_cut + reach_past
    remain = half_row - reach_past
    third_cut = jax.random.randint(jax.random.fold_in(key, 13), (middle_blocks,), jnp.ones((middle_blocks,), jnp.int32), remain, jnp.int32)
    fourth_cut = remain - third_cut
    middle = jnp.stack([lead_cut, crossing, third_cut, fourth_cut], axis=1).reshape(-1)
    tail_five = jax.random.randint(jax.random.fold_in(key, 14), (5,), 1, half_row // 6 + 1, jnp.int32)
    tail_last = half_row - jnp.sum(tail_five)
    leading = jnp.array([half_row, ROW_TOKENS], jnp.int32)
    return jnp.concatenate([leading, middle, tail_five, tail_last.reshape(1)]).astype(jnp.int32)


def with_ends(values, rng, low, largest):
    place = [jax.random.randint(jax.random.fold_in(rng, axis), (), 0, length) for axis, length in enumerate(values.shape)]
    longest = values.shape.index(max(values.shape))
    beside = place[:longest] + [(place[longest] + 1) % values.shape[longest]] + place[longest + 1:]
    return values.at[tuple(place)].set(low).at[tuple(beside)].set(largest)


def block_levels(stream_key, extent, cuts, smallest, high):
    level = 1.0
    for dim, blocks in cuts:
        steps = jax.random.uniform(jax.random.fold_in(jax.random.fold_in(stream_key, 6), dim), (blocks,), jnp.float32, smallest / len(cuts), high / len(cuts))
        level = level * jnp.repeat(jnp.exp(steps), extent[dim] // blocks).reshape((-1,) + (1,) * (len(extent) - 1 - dim))
    return level


def shared_out(rng, own, number, rows, amount, top, most, skew):
    sequence = jax.random.permutation(rng, amount)
    crowded, ordinary = portions_of(amount, rows * top, most, skew, True), portions_of(amount, rows * top, most, skew, False)
    places = jnp.arange(amount)

    def named(sizes, turn):
        used = int((sizes > 0).sum())
        fixed = max(1, used // 4)
        passed = fixed + (places - fixed + turn * (used - fixed)) % max(1, amount - fixed)
        return jnp.zeros((amount,), jnp.int32).at[sequence[jnp.where(places < fixed, places, passed)]].set(jnp.asarray(sizes, jnp.int32))

    sizes = jnp.where(number % 4 == 0, named(crowded, number // 4), named(ordinary, number - number // 4 - 1))
    mixed = jax.random.permutation(jax.random.fold_in(own, 3), amount)
    source_of, sink = mixed[0:amount // 2 * 2:2], mixed[1:amount // 2 * 2:2]
    slack = jnp.minimum(sizes[source_of] - 1, most - sizes[sink]) // 2
    slack = jnp.where((source_of == sequence[0]) | (sink == sequence[0]) | (sizes[sink] == 0), 0, jnp.maximum(slack, 0))
    passed = jax.random.randint(jax.random.fold_in(own, 4), (amount // 2,), 0, 1 << 20) % (slack + 1)
    sizes = sizes.at[source_of].add(-passed).at[sink].add(passed)
    members = jnp.searchsorted(jnp.cumsum(sizes), jnp.arange(rows * top), side="right").astype(jnp.int32)
    listing = members.reshape(top, rows).T
    listing = listing[jax.random.permutation(jax.random.fold_in(own, 1), rows)]
    turn = jax.random.randint(jax.random.fold_in(own, 2), (rows, 1), 0, top)
    return jnp.take_along_axis(listing, (jnp.arange(top)[None, :] + turn) % top, axis=1)


def portions_of(amount, total, most, lean, full):
    portions = [(1 << 20) // math.isqrt(rank ** lean) + 1 for rank in range(1, amount + 1)]
    largest = most if full else min(most, max(-(-total // amount), total * portions[0] // sum(portions)))
    least = 1 if total - largest >= amount - 1 else 0
    holding, surplus = [largest] + [least] * (amount - 1), total - largest - least * (amount - 1)
    while surplus > 0:
        candidates = [i for i in range(1, amount) if holding[i] < largest] or [i for i in range(1, amount) if holding[i] < most]
        whole, remaining = sum([portions[i] for i in candidates]), surplus
        for i in candidates:
            addition = min(most - holding[i], max(1, remaining * portions[i] // whole), surplus)
            holding[i] = holding[i] + addition
            surplus = surplus - addition
    return np.array(holding)


def noise(rng, extent, spread, most, pieces=(), held_as=jnp.bfloat16):
    loudness = block_levels(rng, extent, pieces, -0.22, 0.18) if pieces else 1.0
    result = jax.random.normal(rng, extent, jnp.float32) * spread * loudness
    return jnp.minimum(jnp.maximum(result, -most), most).astype(held_as)


def setup_inputs(seed: int = 0) -> dict:
    key_list = jax.random.split(jax.random.key(seed), 15)
    hidden = noise(key_list[0], (TOKENS, D), 1.0, 6.0, ((0, 32),))
    attn_gain = jnp.clip(1.0 + 0.18 * jax.random.normal(key_list[1], (D,), jnp.float32), 0.1, 1.9)
    w_qkv = draw_w_qkv(jax.random.fold_in(key_list[14], 71), 0)
    kv_cache = draw_kv_cache(jax.random.fold_in(key_list[14], 71), 0)
    page_table = jax.random.permutation(key_list[4], POOL_PAGES).astype(jnp.int32)
    lengths = draw_lengths(jax.random.fold_in(key_list[14], 71), 0)
    request_group = with_ends(jax.random.randint(key_list[6], (REQS,), 0, GROUPS), jax.random.fold_in(key_list[6], 1), 0, GROUPS - 1).astype(jnp.int32)
    key_mask = with_ends((jax.random.randint(key_list[7], (TOKENS,), 0, 3) < 2).astype(jnp.int32), jax.random.fold_in(key_list[7], 1), 0, 1)
    o_weight = noise(key_list[8], (HEADS * HD, D), ((PREFIX / (HEADS * HD)) ** 0.5 * HEADS ** -0.5), 3.5)
    moe_gain = jnp.clip(1.0 + 0.18 * jax.random.normal(key_list[9], (D,), jnp.float32), 0.1, 1.9)
    router = draw_router(jax.random.fold_in(key_list[14], 71), 0)
    routes_keys = jax.random.split(jax.random.fold_in(key_list[11], 1), TOKENS // TOK_DEV)
    routes_turns = jax.random.permutation(jax.random.fold_in(key_list[11], 3), TOKENS // TOK_DEV)
    routes = jax.vmap(lambda own, number: shared_out(jax.random.fold_in(key_list[11], 2), own, number, TOK_DEV, EXPERTS, TOPK, CAP, 2))(routes_keys, routes_turns).reshape((TOKENS, TOPK))
    w_gate_up = noise(key_list[12], (EXPERTS, D, 2 * FFE), (D // 2) ** -0.5, 0.21875, ((0, 16),))
    w_down = noise(key_list[13], (EXPERTS, FFE, D), (FFE // 4) ** -0.5, 0.5, ((0, 16),))
    return {"hidden": hidden, "attn_gain": attn_gain, "w_qkv": w_qkv, "kv_cache": kv_cache, "page_table": page_table, "lengths": lengths, "request_group": request_group, "key_mask": key_mask, "o_weight": o_weight, "moe_gain": moe_gain, "router": router, "routes": routes, "w_gate_up": w_gate_up, "w_down": w_down}


EPSILON = 1e-06
ROPE_BASE = 10000.0
MASKED = -1e+30

def rms_scale(states, gain_vec):
    widened = states.astype(jnp.float32)
    return widened * lax.rsqrt(lax.optimization_barrier(jnp.mean(widened * widened, axis=-1, keepdims=True)) + EPSILON) * gain_vec

def rotate(states, position):
    half_dim = states.shape[-1] // 2
    inv_freq = ROPE_BASE ** (-2.0 * jnp.arange(half_dim, dtype=jnp.float32) / (2 * half_dim))
    angles = position[:, None] * inv_freq[None, :]
    cosine = jnp.cos(angles)[:, None, :]
    sine_part = jnp.sin(angles)[:, None, :]
    lower_half = states[..., :half_dim]
    upper_half = states[..., half_dim:]
    return jnp.concatenate([lower_half * cosine - upper_half * sine_part, upper_half * cosine + lower_half * sine_part], axis=-1)

def token_info(token_ids, lengths, request_group):
    starts = (jnp.cumsum(lengths) - lengths).astype(jnp.int32)
    request = (lax.optimization_barrier(jnp.sum((starts[None, :] <= token_ids[:, None]).astype(jnp.int32), axis=1)) - 1).astype(jnp.int32)
    member = request[:, None] == jnp.arange(starts.shape[0], dtype=jnp.int32)[None, :]
    start_of = lax.optimization_barrier(jnp.sum(jnp.where(member, starts[None, :], 0), axis=1)).astype(jnp.int32)
    group_of = lax.optimization_barrier(jnp.sum(jnp.where(member, request_group[None, :], 0), axis=1)).astype(jnp.int32)
    return (request, start_of, group_of)

def page_groups(page_table):
    n_pages = page_table.shape[0]
    slot_group = jnp.arange(n_pages, dtype=jnp.int32) // (n_pages // GROUPS)
    member = page_table[:, None] == jnp.arange(n_pages, dtype=jnp.int32)[None, :]
    return lax.optimization_barrier(jnp.sum(jnp.where(member, slot_group[:, None], 0), axis=0)).astype(jnp.int32)

def settle(states):
    return lax.optimization_barrier(states.astype(jnp.bfloat16)).astype(jnp.float32)

def reference(hidden, attn_gain, w_qkv, kv_cache, page_table, lengths, request_group, key_mask, o_weight, moe_gain, router, routes, w_gate_up, w_down):
    group_heads = HEADS // KVH
    score_scale = HD ** (-0.5)
    token_ids = jnp.arange(TOKENS, dtype=jnp.int32)
    request, start_of, group_of = token_info(token_ids, lengths, request_group)
    position = (PREFIX + token_ids - start_of).astype(jnp.float32)
    normed = rms_scale(hidden, attn_gain).astype(jnp.bfloat16)
    projected = jnp.dot(normed, w_qkv, preferred_element_type=jnp.float32).reshape(TOKENS, KVH, group_heads + 2, HD)
    queries = rotate(projected[:, :, :group_heads].reshape(TOKENS, HEADS, HD), position).reshape(TOKENS, KVH, group_heads, HD).astype(jnp.bfloat16)
    keys_rot = rotate(projected[:, :, group_heads], position).astype(jnp.bfloat16)
    values_raw = projected[:, :, group_heads + 1].astype(jnp.bfloat16)
    queries, keys_rot, values_raw = lax.optimization_barrier((queries, keys_rot, values_raw))
    pool = kv_cache.reshape(GROUPS * PREFIX, KVH, 2, HD).astype(jnp.float32)
    pool_key = pool[:, :, 0]
    pool_value = pool[:, :, 1]
    pool_group = jnp.repeat(page_groups(page_table), PAGE)
    reach = ROW_TOKENS
    key_pad = jnp.concatenate([jnp.zeros((reach, KVH, HD), jnp.bfloat16), keys_rot], axis=0)
    value_pad = jnp.concatenate([jnp.zeros((reach, KVH, HD), jnp.bfloat16), values_raw], axis=0)
    request_pad = jnp.concatenate([jnp.full((reach,), -1, jnp.int32), request])
    mask_pad = jnp.concatenate([jnp.zeros((reach,), jnp.int32), key_mask.astype(jnp.int32)])
    block = math.gcd(512, TOKENS)

    def attend(index):
        row_first = (index * block).astype(jnp.int32)
        query_block = lax.dynamic_slice_in_dim(queries, row_first, block).astype(jnp.float32)
        block_ids = lax.dynamic_slice_in_dim(token_ids, row_first, block)
        block_request = lax.dynamic_slice_in_dim(request, row_first, block)
        block_group = lax.dynamic_slice_in_dim(group_of, row_first, block)
        window_keys = lax.dynamic_slice_in_dim(key_pad, row_first, block + reach).astype(jnp.float32)
        window_values = lax.dynamic_slice_in_dim(value_pad, row_first, block + reach).astype(jnp.float32)
        window_request = lax.dynamic_slice_in_dim(request_pad, row_first, block + reach)
        window_mask = lax.dynamic_slice_in_dim(mask_pad, row_first, block + reach)
        window_pos = row_first - reach + jnp.arange(block + reach, dtype=jnp.int32)
        pre_scores = jnp.einsum('tgqd,ngd->tgqn', query_block, pool_key) * score_scale
        suf_scores = jnp.einsum('tgqd,ngd->tgqn', query_block, window_keys) * score_scale
        pre_ok = block_group[:, None] == pool_group[None, :]
        suf_ok = (window_request[None, :] == block_request[:, None]) & (window_pos[None, :] <= block_ids[:, None]) & (window_mask[None, :] == 1)
        allowed = jnp.concatenate([pre_ok, suf_ok], axis=1)[:, None, None, :]
        scores = jnp.where(allowed, jnp.concatenate([pre_scores, suf_scores], axis=-1), MASKED)
        peak = lax.optimization_barrier(jnp.max(scores, axis=-1, keepdims=True))
        weights = jnp.where(allowed, jnp.exp(scores - peak), 0.0)
        weights = settle(weights / lax.optimization_barrier(jnp.sum(weights, axis=-1, keepdims=True)))
        context = jnp.einsum('tgqn,ngd->tgqd', weights, jnp.concatenate([pool_value, window_values], axis=0))
        return context.astype(jnp.bfloat16).reshape(block, HEADS * HD)
    context = lax.map(attend, jnp.arange(TOKENS // block, dtype=jnp.int32)).reshape(TOKENS, HEADS * HD)
    attn_branch = jnp.dot(context, o_weight, preferred_element_type=jnp.float32).astype(jnp.bfloat16)
    mid_states = settle(hidden.astype(jnp.float32) + settle(attn_branch))
    mixed = rms_scale(mid_states, moe_gain).astype(jnp.bfloat16)
    logits = jnp.dot(mixed, router, preferred_element_type=jnp.float32)
    picked = jnp.take_along_axis(logits, routes, axis=1)
    gate_probs = jax.nn.softmax(picked, axis=-1)
    limit = TOKENS // TOK_DEV * CAP

    def expert_step(total, expert_id):
        route_hits = routes == expert_id
        gate_e = lax.optimization_barrier(jnp.sum(jnp.where(route_hits, gate_probs, 0.0), axis=1))
        chosen = jnp.any(route_hits, axis=1)
        row_ids = jnp.nonzero(chosen, size=limit, fill_value=0)[0].astype(jnp.int32)
        is_live = jnp.arange(limit, dtype=jnp.int32) < jnp.sum(chosen.astype(jnp.int32)).astype(jnp.int32)
        row_data = mixed[row_ids]
        joined = jnp.dot(row_data, w_gate_up[expert_id], preferred_element_type=jnp.float32)
        activated = (jax.nn.silu(joined[:, :FFE]) * joined[:, FFE:]).astype(jnp.bfloat16)
        expert_out = settle(jnp.dot(activated, w_down[expert_id], preferred_element_type=jnp.float32))
        addend = jnp.where(is_live[:, None], gate_e[row_ids][:, None] * expert_out, 0.0)
        return (total.at[row_ids].add(addend), None)
    routed_sum, _ = lax.scan(expert_step, jnp.zeros((TOKENS, D), jnp.float32), jnp.arange(EXPERTS, dtype=jnp.int32))
    layer_out = (mid_states + routed_sum).astype(jnp.bfloat16)
    return (attn_branch, layer_out)
```

```python
import jax
import jax.numpy as jnp
from jax import lax
from jax.experimental import pallas as pl
from jax.experimental.pallas import tpu as pltpu
from jax.sharding import PartitionSpec as P

D = 1536
HEADS = 24
KVH = 8
HD = 64
FFE = 512
TOPK = 8
PREFIX = 2048
GROUPS = 2
PAGE = 16


EPSILON = 1e-06
ROPE_BASE = 10000.0
MASKED = -1e30


def shifted(array, axis, by):
    count = lax.axis_size(axis)
    pairs = [(i, i + by) for i in range(count) if 0 <= i + by < count]
    return lax.ppermute(array, axis, pairs)


def rms_scale(states, gain_vec):
    widened = states.astype(jnp.float32)
    return (
        widened
        * lax.rsqrt(jnp.mean(widened * widened, axis=-1, keepdims=True) + EPSILON)
        * gain_vec
    )


def rotate(states, position):
    half_dim = states.shape[-1] // 2
    inv_freq = ROPE_BASE ** (-2.0 * jnp.arange(half_dim, dtype=jnp.float32) / (2 * half_dim))
    angles = position[:, None] * inv_freq[None, :]
    cosine = jnp.cos(angles)[:, None, :]
    sine_part = jnp.sin(angles)[:, None, :]
    lower_half = states[..., :half_dim]
    upper_half = states[..., half_dim:]
    return jnp.concatenate(
        [
            lower_half * cosine - upper_half * sine_part,
            upper_half * cosine + lower_half * sine_part,
        ],
        axis=-1,
    )


def token_info(token_ids, lengths, request_group):
    starts = jnp.cumsum(lengths) - lengths
    request = jnp.sum((starts[None, :] <= token_ids[:, None]).astype(jnp.int32), axis=1) - 1
    member = request[:, None] == jnp.arange(starts.shape[0], dtype=jnp.int32)[None, :]
    start_of = jnp.sum(jnp.where(member, starts[None, :], 0), axis=1)
    group_of = jnp.sum(jnp.where(member, request_group[None, :], 0), axis=1)
    return (request, start_of, group_of)


def page_groups(page_table):
    n_pages = page_table.shape[0]
    slot_group = jnp.arange(n_pages, dtype=jnp.int32) // (n_pages // GROUPS)
    member = page_table[:, None] == jnp.arange(n_pages, dtype=jnp.int32)[None, :]
    return jnp.sum(jnp.where(member, slot_group[:, None], 0), axis=0)


def absorb(carry, queries, keys_values, allowed_keys):
    running, denominator, numerator = carry
    scores = jnp.einsum(
        "tgqd,ngd->tgqn", queries, keys_values[:, :, 0], preferred_element_type=jnp.float32
    ) * HD ** (-0.5)
    allowed = allowed_keys[:, None, None, :]
    scores = jnp.where(allowed, scores, MASKED)
    new_running = jnp.maximum(running, jnp.max(scores, axis=-1))
    weights = jnp.where(allowed, jnp.exp(scores - new_running[..., None]), 0.0)
    rescale = jnp.exp(running - new_running)
    denominator = denominator * rescale + jnp.sum(weights, axis=-1)
    numerator = numerator * rescale[..., None] + jnp.einsum(
        "tgqn,ngd->tgqd",
        weights.astype(jnp.bfloat16),
        keys_values[:, :, 1],
        preferred_element_type=jnp.float32,
    )
    return (new_running, denominator, numerator)


def absorb_blocks(carry, queries, keys_values, allowed_keys):
    key_count = keys_values.shape[0]
    width_block = min(key_count, 1024)
    for offset in range(0, key_count, width_block):
        carry = absorb(
            carry,
            queries,
            keys_values[offset : offset + width_block],
            allowed_keys[:, offset : offset + width_block],
        )
    return carry


LANES = 128


def crossed(array, axis, flip):
    count = lax.axis_size(axis)
    return lax.ppermute(array, axis, [(i, i ^ flip) for i in range(count)])


def spread(own, axis):
    count = lax.axis_size(axis)
    slots = {0: own}
    bit = count // 2
    while bit:
        for d in sorted(slots):
            slots[d | bit] = crossed(slots[d], axis, bit)
        bit //= 2
    return slots


def folded(parts, axis):
    count = lax.axis_size(axis)
    parts = dict(parts)
    bit = 1
    while bit < count:
        for d in sorted(parts, reverse=True):
            if d & bit:
                came = crossed(parts.pop(d).astype(jnp.bfloat16), axis, bit)
                parts[d ^ bit] = parts[d ^ bit].astype(jnp.float32) + came.astype(jnp.float32)
        bit *= 2
    return parts[0]


def expert_kernel(count, experts_here, where_ref, *refs):
    state_refs = refs[:count]
    hits_ref, router_ref, up_ref, down_ref = refs[count : count + 4]
    out_refs = refs[count + 4 :]
    me = where_ref[0]
    rows = state_refs[0].shape[0]
    states = jnp.concatenate([ref[...] for ref in state_refs], axis=0)
    hits = jnp.concatenate(
        [
            hits_ref[pl.ds(pl.multiple_of(where_ref[1 + i] * rows, rows), rows), :]
            for i in range(count)
        ],
        axis=0,
    )
    logits = jnp.dot(states, router_ref[...], preferred_element_type=jnp.float32)
    hit = hits.astype(jnp.float32) > 0.0
    logits = jnp.where(hit, logits, MASKED)
    peak = jnp.max(logits, axis=-1, keepdims=True)
    shares = jnp.where(hit, jnp.exp(logits - peak), 0.0)
    total = jnp.sum(shares, axis=-1, keepdims=True)
    lane = lax.broadcasted_iota(jnp.int32, shares.shape, 1)
    result = None
    for x in range(experts_here):
        mine = jnp.sum(jnp.where(lane == me * experts_here + x, shares, 0.0), axis=-1, keepdims=True)
        gate = mine / total
        joined = jnp.dot(states, up_ref[x], preferred_element_type=jnp.float32)
        lead = joined[:, :FFE]
        activated = (lead / (1.0 + jnp.exp(-lead)) * joined[:, FFE:]).astype(jnp.bfloat16)
        part = gate * jnp.dot(activated, down_ref[x], preferred_element_type=jnp.float32)
        result = part if result is None else result + part
    for i in range(count):
        out_refs[i][...] = result[i * rows : (i + 1) * rows].astype(jnp.bfloat16)


def run_experts(slots, offsets, me, hits, router, w_gate_up, w_down):
    count = len(offsets)
    where = jnp.stack([me] + [me ^ d for d in offsets]).astype(jnp.int32)
    vmem = pl.BlockSpec(memory_space=pltpu.VMEM)
    outs = pl.pallas_call(
        lambda *refs: expert_kernel(count, w_gate_up.shape[0], *refs),
        out_shape=[jax.ShapeDtypeStruct(slots[d].shape, jnp.bfloat16) for d in offsets],
        in_specs=[pl.BlockSpec(memory_space=pltpu.SMEM)] + [vmem] * (count + 4),
        out_specs=[vmem] * count,
        compiler_params=pltpu.CompilerParams(vmem_limit_bytes=56 << 20),
        name="experts",
    )(where, *[slots[d] for d in offsets], hits, router, w_gate_up, w_down)
    return dict(zip(offsets, outs))


def per_device(
    hidden,
    attn_gain,
    w_qkv,
    kv_cache,
    page_table,
    lengths,
    request_group,
    key_mask,
    o_weight,
    moe_gain,
    router,
    routes,
    w_gate_up,
    w_down,
):
    n_tok = lax.axis_size("tok")
    n_head = lax.axis_size("head")
    tok_dev = hidden.shape[0]
    row_tokens = tok_dev * n_head
    group_heads = HEADS // KVH
    kv_dev = w_qkv.shape[1] // ((group_heads + 2) * HD)
    heads_dev = kv_dev * group_heads
    row_index = lax.axis_index("tok")
    head_index = lax.axis_index("head")
    row_states = lax.all_gather(hidden, "head", axis=0, tiled=True)
    normed = rms_scale(row_states, attn_gain).astype(jnp.bfloat16)
    projected = jnp.dot(normed, w_qkv, preferred_element_type=jnp.float32).reshape(
        row_tokens, kv_dev, group_heads + 2, HD
    )
    row_first = row_index * row_tokens
    own_index = row_first + jnp.arange(row_tokens, dtype=jnp.int32)
    own_request, own_start, own_group = token_info(own_index, lengths, request_group)
    position = (PREFIX + own_index - own_start).astype(jnp.float32)
    queries = (
        rotate(projected[:, :, :group_heads].reshape(row_tokens, heads_dev, HD), position)
        .reshape(row_tokens, kv_dev, group_heads, HD)
        .astype(jnp.bfloat16)
    )
    keys_rot = rotate(projected[:, :, group_heads], position)
    values_raw = projected[:, :, group_heads + 1]
    own_kv = (
        jnp.stack([keys_rot, values_raw], axis=2)
        .astype(jnp.bfloat16)
        .reshape(row_tokens, kv_dev * 2 * HD)
    )
    prior_kv = shifted(own_kv, "tok", 1)
    window = jnp.concatenate([prior_kv, own_kv], axis=0).reshape(2 * row_tokens, kv_dev, 2, HD)
    window_pos = row_first - row_tokens + jnp.arange(2 * row_tokens, dtype=jnp.int32)
    window_request = token_info(jnp.maximum(window_pos, 0), lengths, request_group)[0]
    mask_padded = jnp.concatenate([jnp.zeros((row_tokens,), jnp.int32), key_mask])
    window_mask = lax.dynamic_slice_in_dim(mask_padded, row_first, 2 * row_tokens)
    suffix_allowed = (
        ((window_pos >= 0) & (window_mask == 1))[None, :]
        & (window_request[None, :] == own_request[:, None])
        & (window_pos[None, :] <= own_index[:, None])
    )
    page_group = page_groups(page_table)
    n_pages = page_table.shape[0]
    start_carry = (
        jnp.full((row_tokens, kv_dev, group_heads), MASKED, jnp.float32),
        jnp.zeros((row_tokens, kv_dev, group_heads), jnp.float32),
        jnp.zeros((row_tokens, kv_dev, group_heads, HD), jnp.float32),
    )
    piece = lax.all_gather(kv_cache, "tok", axis=0, tiled=True)
    key_count = piece.shape[0]
    page_of = jnp.arange(key_count, dtype=jnp.int32) // PAGE
    member = page_of[:, None] == jnp.arange(n_pages, dtype=jnp.int32)[None, :]
    piece_group = jnp.sum(jnp.where(member, page_group[None, :], 0), axis=1)
    allowed_keys = own_group[:, None] == piece_group[None, :]
    carry = absorb_blocks(
        start_carry, queries, piece.reshape(key_count, kv_dev, 2, HD), allowed_keys
    )
    running, denominator, numerator = absorb_blocks(carry, queries, window, suffix_allowed)
    context = (
        (numerator / denominator[..., None])
        .astype(jnp.bfloat16)
        .reshape(row_tokens, heads_dev * HD)
    )
    rows_out = lax.dynamic_slice_in_dim(o_weight, head_index * heads_dev * HD, heads_dev * HD, 0)
    attn_sum = lax.psum_scatter(
        jnp.dot(context, rows_out, preferred_element_type=jnp.float32).astype(jnp.bfloat16),
        "head",
        scatter_dimension=0,
        tiled=True,
    )
    mid_states = (hidden.astype(jnp.float32) + attn_sum.astype(jnp.float32)).astype(jnp.bfloat16)
    mixed = rms_scale(mid_states, moe_gain).astype(jnp.bfloat16)
    experts = router.shape[1]
    lanes = -(-experts // LANES) * LANES
    all_routes = lax.all_gather(routes, "tok", axis=0, tiled=True)
    hits = jnp.any(
        all_routes[:, :, None] == jnp.arange(lanes, dtype=jnp.int32)[None, None, :], axis=1
    ).astype(jnp.bfloat16)
    wide_router = jnp.pad(router, ((0, 0), (0, lanes - experts)))
    slots = spread(mixed, "tok")
    together = min(4, n_tok)
    parts = {}
    for first in range(0, n_tok, together):
        parts.update(
            run_experts(
                slots,
                list(range(first, first + together)),
                row_index,
                hits,
                wide_router,
                w_gate_up,
                w_down,
            )
        )
    routed_sum = folded(parts, "tok").astype(jnp.float32)
    layer_out = (mid_states.astype(jnp.float32) + routed_sum).astype(jnp.bfloat16)
    return (attn_sum, layer_out)


def solution(mesh):
    return jax.shard_map(
        per_device,
        mesh=mesh,
        in_specs=(
            P(("tok", "head"), None),
            P(),
            P(None, "head"),
            P("tok", "head"),
            P(),
            P(),
            P(),
            P(),
            P(),
            P(),
            P(),
            P(("tok", "head"), None),
            P("tok", None, None),
            P("tok", None, None),
        ),
        out_specs=(P(("tok", "head"), None), P(("tok", "head"), None)),
        check_vma=False,
    )
```

```python
import functools

import jax
import jax.numpy as jnp
from jax import lax
from jax.experimental import pallas as pl
from jax.experimental.pallas import tpu as pltpu
from jax.sharding import PartitionSpec as P

D = 1536
HEADS = 24
KVH = 8
HD = 64
FFE = 512
TOPK = 8
PREFIX = 2048
GROUPS = 2
PAGE = 16
QPG = HEADS // KVH
BLOCK = 64


EPSILON = 1e-06
ROPE_BASE = 10000.0
MASKED = -1e30

LANES = 128


def crossed(array, axis, flip):
    count = lax.axis_size(axis)
    return lax.ppermute(array, axis, [(i, i ^ flip) for i in range(count)])


def spread(own, axis):
    count = lax.axis_size(axis)
    slots = {0: own}
    bit = count // 2
    while bit:
        for d in sorted(slots):
            slots[d | bit] = crossed(slots[d], axis, bit)
        bit //= 2
    return slots


def folded(parts, axis):
    count = lax.axis_size(axis)
    parts = dict(parts)
    bit = 1
    while bit < count:
        for d in sorted(parts, reverse=True):
            if d & bit:
                came = crossed(parts.pop(d).astype(jnp.bfloat16), axis, bit)
                parts[d ^ bit] = parts[d ^ bit].astype(jnp.float32) + came.astype(jnp.float32)
        bit *= 2
    return parts[0]


VMEM = pl.BlockSpec(memory_space=pltpu.VMEM)
SMEM = pl.BlockSpec(memory_space=pltpu.SMEM)
PARAMS = pltpu.CompilerParams(vmem_limit_bytes=56 << 20)


def token_info(token_ids, lengths, request_group):
    ends = jnp.cumsum(lengths)
    starts = ends - lengths
    member = (starts[None, :] <= token_ids[:, None]) & (token_ids[:, None] < ends[None, :])
    request = jnp.sum(
        jnp.where(member, jnp.arange(lengths.shape[0], dtype=jnp.int32)[None, :], 0), axis=1
    )
    start_of = jnp.sum(jnp.where(member, starts[None, :], 0), axis=1)
    group_of = jnp.sum(jnp.where(member, request_group[None, :], 0), axis=1)
    return (request, start_of, group_of)


def ranks(group_of):
    count = group_of.shape[0]
    order = group_of * count + jnp.arange(count, dtype=jnp.int32)
    rank = jnp.sum((order[None, :] < order[:, None]).astype(jnp.int32), axis=1)
    return rank, jnp.sum((group_of == 0).astype(jnp.int32))


def arranged(values, rank):
    count = rank.shape[0]
    place = rank[None, :] == jnp.arange(count, dtype=jnp.int32)[:, None]
    return jnp.sum(jnp.where(place, values[None, :], 0), axis=1)


def project_kernel(slots, kv_dev, rank_ref, gain_ref, weight_ref, cos_ref, sin_ref, *refs):
    state_refs = refs[:slots]
    query_ref, kv_ref = refs[slots:]
    states = jnp.concatenate([ref[...] for ref in state_refs], axis=0).astype(jnp.float32)
    rows = states.shape[0]
    scale = lax.rsqrt(jnp.mean(states * states, axis=-1, keepdims=True) + EPSILON)
    normed = (states * scale * gain_ref[...]).astype(jnp.bfloat16)
    place = rank_ref[...] == lax.broadcasted_iota(jnp.int32, (rows, rows), 0)
    normed = jnp.dot(
        place.astype(jnp.bfloat16), normed, preferred_element_type=jnp.float32
    ).astype(jnp.bfloat16)
    projected = jnp.dot(normed, weight_ref[...], preferred_element_type=jnp.float32)
    cosine = cos_ref[...]
    sine = sin_ref[...]
    lane = lax.broadcasted_iota(jnp.int32, (rows, LANES), 1)
    low = lane < HD
    first = lane % HD < HD // 2

    def tile(number):
        return projected[:, number * LANES : (number + 1) * LANES]

    @functools.cache
    def turned(number):
        plain = tile(number)
        partner = jnp.where(
            first, pltpu.roll(plain, LANES - HD // 2, 1), pltpu.roll(plain, HD // 2, 1)
        )
        return plain * cosine + partner * sine

    for j in range(kv_dev):
        unit = j * (QPG + 2)
        for i in range(QPG):
            query = turned((unit + i) // 2)
            if (unit + i) % 2:
                query = pltpu.roll(query, HD, 1)
            query_ref[j, i] = jnp.where(low, query * HD ** (-0.5), 0.0).astype(jnp.bfloat16)
        key, value = turned((unit + QPG) // 2), tile((unit + QPG + 1) // 2)
        if (unit + QPG) % 2:
            key, value = pltpu.roll(key, HD, 1), pltpu.roll(value, HD, 1)
        kv_ref[:, j * LANES : (j + 1) * LANES] = jnp.where(low, key, value).astype(jnp.bfloat16)


def scored(queries, keys):
    return lax.dot_general(
        queries, keys, (((1,), (1,)), ((), ())), preferred_element_type=jnp.float32
    )


def attend_kernel(
    shards,
    kv_dev,
    slots,
    scalar_ref,
    place_ref,
    query_ref,
    prior_ref,
    own_ref,
    row_request_ref,
    row_id_ref,
    key_request_ref,
    key_id_ref,
    rank_ref,
    *refs,
):
    shard_refs = refs[:shards]
    out_refs = refs[shards : shards + slots]
    pool_ref, peak_ref, total_ref, sum_ref, arrived = refs[shards + slots :]
    me = scalar_ref[0]
    in_first = scalar_ref[1]
    rows = query_ref.shape[2]
    blocks = rows // BLOCK
    shard_pages = shard_refs[0].shape[0] // PAGE

    for d in range(shards):
        def start(j, carry, d=d):
            page = (me ^ d) * shard_pages + j
            pltpu.make_async_copy(
                shard_refs[d].at[pl.ds(pl.multiple_of(j * PAGE, PAGE), PAGE), :],
                pool_ref.at[pl.ds(pl.multiple_of(place_ref[page] * PAGE, PAGE), PAGE), :],
                arrived,
            ).start()
            return carry

        lax.fori_loop(0, shard_pages, start, 0)

    def near(b, carry):
        at = pl.ds(pl.multiple_of(b * BLOCK, BLOCK), BLOCK)
        request = row_request_ref[at, :]
        ident = row_id_ref[at, :]
        allowed = (key_request_ref[...] == request) & (key_id_ref[...] <= ident)
        allowed = jnp.concatenate([allowed.astype(jnp.float32)] * QPG, axis=0) > 0.0
        for j in range(kv_dev):
            queries = query_ref[j, :, at, :].reshape(QPG * BLOCK, LANES)
            columns = slice(j * LANES, (j + 1) * LANES)
            keys = jnp.concatenate([prior_ref[:, columns], own_ref[:, columns]], axis=0)
            scores = jnp.where(allowed, scored(queries, keys), MASKED)
            peak = jnp.max(scores, axis=-1, keepdims=True)
            weights = jnp.where(allowed, jnp.exp(scores - peak), 0.0)
            total = jnp.sum(weights, axis=-1, keepdims=True)
            mixed = jnp.dot(
                weights.astype(jnp.bfloat16), keys, preferred_element_type=jnp.float32
            )
            shape = (QPG, BLOCK, LANES)
            peak_ref[j, :, at, :] = jnp.broadcast_to(peak, mixed.shape).reshape(shape)
            total_ref[j, :, at, :] = jnp.broadcast_to(total, mixed.shape).reshape(shape)
            sum_ref[j, :, at, :] = mixed.reshape(shape)
        return carry

    lax.fori_loop(0, blocks, near, 0)
    pltpu.make_async_copy(pool_ref, pool_ref, arrived).wait()

    group_rows = pool_ref.shape[0] // GROUPS
    full = (in_first + BLOCK - 1) // BLOCK
    skip = in_first // BLOCK

    def far(item, carry):
        group = (item >= full).astype(jnp.int32)
        b = jnp.where(item < full, item, item - full + skip)
        at = pl.ds(pl.multiple_of(b * BLOCK, BLOCK), BLOCK)
        keys_at = pl.ds(pl.multiple_of(group * group_rows, group_rows), group_rows)
        line = lax.broadcasted_iota(jnp.int32, (QPG, BLOCK, LANES), 1) + b * BLOCK
        chosen = (line >= in_first) == (group == 1)
        shape = (QPG, BLOCK, LANES)
        for j in range(kv_dev):
            queries = query_ref[j, :, at, :].reshape(QPG * BLOCK, LANES)
            keys = pool_ref[keys_at, j * LANES : (j + 1) * LANES]
            scores = scored(queries, keys)
            here = jnp.max(scores, axis=-1, keepdims=True)
            weights = jnp.exp(scores - here)
            total = jnp.sum(weights, axis=-1, keepdims=True)
            mixed = jnp.dot(
                weights.astype(jnp.bfloat16), keys, preferred_element_type=jnp.float32
            ).reshape(shape)
            here = jnp.broadcast_to(here, (QPG * BLOCK, LANES)).reshape(shape)
            total = jnp.broadcast_to(total, (QPG * BLOCK, LANES)).reshape(shape)
            before = peak_ref[j, :, at, :]
            peak = jnp.maximum(before, here)
            keep, gain = jnp.exp(before - peak), jnp.exp(here - peak)
            joint_total = total_ref[j, :, at, :] * keep + total * gain
            joint_sum = sum_ref[j, :, at, :] * keep + mixed * gain
            total_ref[j, :, at, :] = jnp.where(chosen, joint_total, total_ref[j, :, at, :])
            sum_ref[j, :, at, :] = jnp.where(chosen, joint_sum, sum_ref[j, :, at, :])
        return carry

    lax.fori_loop(0, full + blocks - skip, far, 0)

    back = (rank_ref[...] == lax.broadcasted_iota(jnp.int32, (rows, rows), 1)).astype(jnp.bfloat16)
    lane = lax.broadcasted_iota(jnp.int32, (rows, LANES), 1)
    piece = rows // slots
    heads = [
        sum_ref[j, i] / total_ref[j, i] for j in range(kv_dev) for i in range(QPG)
    ]
    for h in range(0, len(heads), 2):
        pair = pltpu.roll(heads[h], HD, 1)
        if h + 1 < len(heads):
            pair = jnp.where(lane < HD, pair, heads[h + 1])
        pair = jnp.dot(
            back, pair.astype(jnp.bfloat16), preferred_element_type=jnp.float32
        ).astype(jnp.bfloat16)
        width = min(LANES, len(heads) * HD - h * HD)
        for k in range(slots):
            out_refs[k][:, h * HD : h * HD + width] = pair[k * piece : (k + 1) * piece, :width]


def close_kernel(slots, scalar_ref, hidden_ref, weight_ref, gain_ref, *refs):
    context_refs = refs[:slots]
    branch_ref, mid_ref, mixed_ref = refs[slots:]
    width = context_refs[0].shape[1]
    total = None
    for k in range(slots):
        first = pl.multiple_of((scalar_ref[0] ^ k) * width, width)
        part = jnp.dot(
            context_refs[k][...],
            weight_ref[pl.ds(first, width), :],
            preferred_element_type=jnp.float32,
        )
        total = part if total is None else total + part
    branch = total.astype(jnp.bfloat16)
    branch_ref[...] = branch
    mid = (hidden_ref[...].astype(jnp.float32) + branch.astype(jnp.float32)).astype(jnp.bfloat16)
    mid_ref[...] = mid
    wide = mid.astype(jnp.float32)
    scale = lax.rsqrt(jnp.mean(wide * wide, axis=-1, keepdims=True) + EPSILON)
    mixed_ref[...] = (wide * scale * gain_ref[...]).astype(jnp.bfloat16)


def expert_kernel(count, experts_here, where_ref, *refs):
    state_refs = refs[:count]
    routes_ref, router_ref, up_ref, down_ref = refs[count : count + 4]
    out_refs = refs[count + 4 :]
    me = where_ref[0]
    rows = state_refs[0].shape[0]
    lanes = router_ref.shape[1]
    states = jnp.concatenate([ref[...] for ref in state_refs], axis=0)
    lane = lax.broadcasted_iota(jnp.int32, (rows, lanes), 1)
    hits = []
    for i in range(count):
        first = pl.multiple_of(where_ref[1 + i] * TOPK, TOPK)
        routes = jnp.transpose(routes_ref[pl.ds(first, TOPK), :].astype(jnp.float32)).astype(jnp.int32)
        hit = jnp.zeros((rows, lanes), jnp.float32)
        for k in range(TOPK):
            hit = jnp.where(lane == routes[:, k : k + 1], 1.0, hit)
        hits.append(hit)
    hit = jnp.concatenate(hits, axis=0) > 0.0
    logits = jnp.dot(states, router_ref[...], preferred_element_type=jnp.float32)
    logits = jnp.where(hit, logits, MASKED)
    peak = jnp.max(logits, axis=-1, keepdims=True)
    shares = jnp.where(hit, jnp.exp(logits - peak), 0.0)
    total = jnp.sum(shares, axis=-1, keepdims=True)
    lane = lax.broadcasted_iota(jnp.int32, shares.shape, 1)
    result = None
    for x in range(experts_here):
        mine = jnp.sum(jnp.where(lane == me * experts_here + x, shares, 0.0), axis=-1, keepdims=True)
        gate = mine / total
        joined = jnp.dot(states, up_ref[x], preferred_element_type=jnp.float32)
        lead = joined[:, :FFE]
        activated = (lead / (1.0 + jnp.exp(-lead)) * joined[:, FFE:]).astype(jnp.bfloat16)
        part = gate * jnp.dot(activated, down_ref[x], preferred_element_type=jnp.float32)
        result = part if result is None else result + part
    for i in range(count):
        out_refs[i][...] = result[i * rows : (i + 1) * rows].astype(jnp.bfloat16)


def run_experts(slots, offsets, me, routes, router, w_gate_up, w_down):
    count = len(offsets)
    where = jnp.stack([me] + [me ^ d for d in offsets]).astype(jnp.int32)
    outs = pl.pallas_call(
        functools.partial(expert_kernel, count, w_gate_up.shape[0]),
        out_shape=[jax.ShapeDtypeStruct(slots[d].shape, jnp.bfloat16) for d in offsets],
        in_specs=[SMEM] + [VMEM] * (count + 4),
        out_specs=[VMEM] * count,
        compiler_params=PARAMS,
        name="experts",
    )(where, *[slots[d] for d in offsets], routes, router, w_gate_up, w_down)
    return dict(zip(offsets, outs))


def per_device(
    hidden,
    attn_gain,
    w_qkv,
    kv_cache,
    page_table,
    lengths,
    request_group,
    key_mask,
    o_weight,
    moe_gain,
    router,
    routes,
    w_gate_up,
    w_down,
):
    n_tok = lax.axis_size("tok")
    n_head = lax.axis_size("head")
    tok_dev = hidden.shape[0]
    row_tokens = tok_dev * n_head
    kv_dev = w_qkv.shape[1] // ((QPG + 2) * HD)
    row_index = lax.axis_index("tok")
    head_index = lax.axis_index("head")

    states = spread(hidden, "head")
    shards = spread(kv_cache, "tok")

    within = jnp.arange(tok_dev, dtype=jnp.int32)
    row_offset = jnp.concatenate(
        [(head_index ^ k).astype(jnp.int32) * tok_dev + within for k in range(n_head)]
    )
    own_ids = row_index * row_tokens + row_offset
    prior_ids = own_ids - row_tokens
    own_request, own_start, own_group = token_info(own_ids, lengths, request_group)
    prior_request, _, prior_group = token_info(prior_ids, lengths, request_group)
    rank, in_first = ranks(own_group)
    prior_rank, _ = ranks(prior_group)
    token_mask = jnp.concatenate([jnp.zeros((row_tokens,), jnp.int32), key_mask])
    window = lax.dynamic_slice_in_dim(token_mask, row_index * row_tokens, 2 * row_tokens)
    window = window.reshape(2 * n_head, tok_dev)
    flipped = [(head_index ^ k) for k in range(n_head)]
    prior_mask = jnp.concatenate([window[f] for f in flipped])
    own_mask = jnp.concatenate([window[n_head + f] for f in flipped])
    ids = arranged(own_ids, rank)
    request = arranged(own_request, rank)
    position = (PREFIX + arranged(own_ids - own_start, rank)).astype(jnp.float32)
    key_request = jnp.concatenate(
        [
            arranged(jnp.where(prior_mask == 1, prior_request, -1), prior_rank),
            arranged(jnp.where(own_mask == 1, own_request, -1), rank),
        ]
    )
    key_ids = jnp.concatenate([arranged(prior_ids, prior_rank), ids])
    half = HD // 2
    inv_freq = ROPE_BASE ** (-2.0 * jnp.arange(half, dtype=jnp.float32) / HD)
    angles = position[:, None] * jnp.tile(inv_freq, LANES // half)[None, :]
    sign = jnp.where(jnp.arange(LANES, dtype=jnp.int32) % HD < half, -1.0, 1.0)
    cosine = jnp.cos(angles)
    sine = jnp.sin(angles) * sign[None, :]
    n_pages = page_table.shape[0]
    pages = jnp.arange(n_pages, dtype=jnp.int32)
    place = jnp.sum(
        jnp.where(page_table[:, None] == pages[None, :], pages[:, None], 0), axis=0
    )
    experts = router.shape[1]
    wide_router = jnp.pad(router, ((0, 0), (0, -experts % LANES)))
    all_routes = lax.all_gather(routes.T, "tok", axis=0, tiled=True)
    all_routes, place, key_request, key_ids, wide_router, cosine, sine = lax.optimization_barrier(
        (all_routes, place, key_request, key_ids, wide_router, cosine, sine)
    )

    columns = w_qkv.shape[1]
    queries, own_kv = pl.pallas_call(
        functools.partial(project_kernel, n_head, kv_dev),
        out_shape=[
            jax.ShapeDtypeStruct((kv_dev, QPG, row_tokens, LANES), jnp.bfloat16),
            jax.ShapeDtypeStruct((row_tokens, kv_dev * LANES), jnp.bfloat16),
        ],
        in_specs=[VMEM] * (5 + n_head),
        out_specs=[VMEM] * 2,
        compiler_params=PARAMS,
        name="project",
    )(
        rank[None, :],
        attn_gain[None, :],
        jnp.pad(w_qkv, ((0, 0), (0, -columns % LANES))),
        cosine,
        sine,
        *[states[k] for k in range(n_head)],
    )
    prior_kv = lax.ppermute(own_kv, "tok", [(i, i + 1) for i in range(n_tok - 1)])
    pool_rows = kv_cache.shape[0] * n_tok
    contexts = pl.pallas_call(
        functools.partial(attend_kernel, n_tok, kv_dev, n_head),
        out_shape=[jax.ShapeDtypeStruct((tok_dev, kv_dev * QPG * HD), jnp.bfloat16)] * n_head,
        in_specs=[SMEM] * 2 + [VMEM] * 8 + [pl.BlockSpec(memory_space=pl.ANY)] * n_tok,
        out_specs=[VMEM] * n_head,
        scratch_shapes=[pltpu.VMEM((pool_rows, kv_cache.shape[1]), jnp.bfloat16)]
        + [pltpu.VMEM((kv_dev, QPG, row_tokens, LANES), jnp.float32)] * 3
        + [pltpu.SemaphoreType.DMA],
        compiler_params=PARAMS,
        name="attend",
    )(
        jnp.stack([row_index, in_first]).astype(jnp.int32),
        place,
        queries,
        prior_kv,
        own_kv,
        request[:, None],
        ids[:, None],
        key_request[None, :],
        key_ids[None, :],
        rank[:, None],
        *[shards[d] for d in range(n_tok)],
    )
    context_slots = [contexts[0]] + [crossed(contexts[k], "head", k) for k in range(1, n_head)]
    attn_sum, mid_states, mixed = pl.pallas_call(
        functools.partial(close_kernel, n_head),
        out_shape=[jax.ShapeDtypeStruct(hidden.shape, jnp.bfloat16)] * 3,
        in_specs=[SMEM] + [VMEM] * (3 + n_head),
        out_specs=[VMEM] * 3,
        compiler_params=PARAMS,
        name="close",
    )(
        head_index.astype(jnp.int32)[None],
        hidden,
        o_weight,
        moe_gain[None, :],
        *context_slots,
    )

    slots = spread(mixed, "tok")
    together = min(4, n_tok)
    parts = {}
    for first in range(0, n_tok, together):
        parts.update(
            run_experts(
                slots,
                list(range(first, first + together)),
                row_index,
                all_routes,
                wide_router,
                w_gate_up,
                w_down,
            )
        )
    routed_sum = folded(parts, "tok").astype(jnp.float32)
    layer_out = (mid_states.astype(jnp.float32) + routed_sum).astype(jnp.bfloat16)
    return (attn_sum, layer_out)


def solution(mesh):
    return jax.shard_map(
        per_device,
        mesh=mesh,
        in_specs=(
            P(("tok", "head"), None),
            P(),
            P(None, "head"),
            P("tok", "head"),
            P(),
            P(),
            P(),
            P(),
            P(),
            P(),
            P(),
            P(("tok", "head"), None),
            P("tok", None, None),
            P("tok", None, None),
        ),
        out_specs=(P(("tok", "head"), None), P(("tok", "head"), None)),
        check_vma=False,
    )
```

```python
import functools

import jax
import jax.numpy as jnp
from jax import lax
from jax.experimental import pallas as pl
from jax.experimental.pallas import tpu as pltpu
from jax.sharding import PartitionSpec as P

D = 1536
HEADS = 24
KVH = 8
HD = 64
FFE = 512
TOPK = 8
PREFIX = 2048
GROUPS = 2
PAGE = 16
QPG = HEADS // KVH
BLOCK = 64


EPSILON = 1e-06
ROPE_BASE = 10000.0
MASKED = -1e30

LANES = 128


def crossed(array, axis, flip):
    count = lax.axis_size(axis)
    return lax.ppermute(array, axis, [(i, i ^ flip) for i in range(count)])


def spread(own, axis, bits):
    slots = {0: own}
    for bit in bits:
        for d in sorted(slots):
            slots[d | bit] = crossed(slots[d], axis, bit)
    return slots


def folded(parts, axis, bits):
    parts = dict(parts)
    for bit in bits:
        for d in sorted(parts, reverse=True):
            if d & bit:
                came = crossed(parts.pop(d).astype(jnp.bfloat16), axis, bit)
                parts[d ^ bit] = parts[d ^ bit].astype(jnp.float32) + came.astype(jnp.float32)
    return parts[0]


def bits_of(count):
    return [1 << i for i in reversed(range(count.bit_length() - 1))]


VMEM = pl.BlockSpec(memory_space=pltpu.VMEM)
SMEM = pl.BlockSpec(memory_space=pltpu.SMEM)
TAIL = 16


def params(mib):
    return pltpu.CompilerParams(vmem_limit_bytes=mib << 20)


def pinned(array):
    return pltpu.with_memory_space_constraint(array, pltpu.VMEM)


def token_info(token_ids, lengths, request_group):
    ends = jnp.cumsum(lengths)
    starts = ends - lengths
    member = (starts[None, :] <= token_ids[:, None]) & (token_ids[:, None] < ends[None, :])
    request = jnp.sum(
        jnp.where(member, jnp.arange(lengths.shape[0], dtype=jnp.int32)[None, :], 0), axis=1
    )
    start_of = jnp.sum(jnp.where(member, starts[None, :], 0), axis=1)
    group_of = jnp.sum(jnp.where(member, request_group[None, :], 0), axis=1)
    return (request, start_of, group_of)


def ranks(group_of):
    count = group_of.shape[0]
    order = group_of * count + jnp.arange(count, dtype=jnp.int32)
    rank = jnp.sum((order[None, :] < order[:, None]).astype(jnp.int32), axis=1)
    return rank, jnp.sum((group_of == 0).astype(jnp.int32))


def arranged(values, rank):
    count = rank.shape[0]
    place = rank[None, :] == jnp.arange(count, dtype=jnp.int32)[:, None]
    return jnp.sum(jnp.where(place, values[None, :], 0), axis=1)


def project_kernel(slots, kv_dev, rank_ref, gain_ref, weight_ref, cos_ref, sin_ref, *refs):
    state_refs = refs[:slots]
    query_ref, kv_ref = refs[slots:]
    states = jnp.concatenate([ref[...] for ref in state_refs], axis=0).astype(jnp.float32)
    rows = states.shape[0]
    scale = lax.rsqrt(jnp.mean(states * states, axis=-1, keepdims=True) + EPSILON)
    normed = (states * scale * gain_ref[...]).astype(jnp.bfloat16)
    place = rank_ref[...] == lax.broadcasted_iota(jnp.int32, (rows, rows), 0)
    normed = jnp.dot(
        place.astype(jnp.bfloat16), normed, preferred_element_type=jnp.float32
    ).astype(jnp.bfloat16)
    projected = jnp.dot(normed, weight_ref[...], preferred_element_type=jnp.float32)
    cosine = cos_ref[...]
    sine = sin_ref[...]
    lane = lax.broadcasted_iota(jnp.int32, (rows, LANES), 1)
    low = lane < HD
    first = lane % HD < HD // 2

    def tile(number):
        return projected[:, number * LANES : (number + 1) * LANES]

    @functools.cache
    def turned(number):
        plain = tile(number)
        partner = jnp.where(
            first, pltpu.roll(plain, LANES - HD // 2, 1), pltpu.roll(plain, HD // 2, 1)
        )
        return plain * cosine + partner * sine

    for j in range(kv_dev):
        unit = j * (QPG + 2)
        for i in range(QPG):
            query = turned((unit + i) // 2)
            if (unit + i) % 2:
                query = pltpu.roll(query, HD, 1)
            query_ref[j, i] = jnp.where(low, query * HD ** (-0.5), 0.0).astype(jnp.bfloat16)
        key, value = turned((unit + QPG) // 2), tile((unit + QPG + 1) // 2)
        if (unit + QPG) % 2:
            key, value = pltpu.roll(key, HD, 1), pltpu.roll(value, HD, 1)
        kv_ref[:, j * LANES : (j + 1) * LANES] = jnp.where(low, key, value).astype(jnp.bfloat16)


def scored(queries, keys):
    return lax.dot_general(
        queries, keys, (((1,), (1,)), ((), ())), preferred_element_type=jnp.float32
    )


def attend_kernel(
    shards,
    kv_dev,
    slots,
    scalar_ref,
    place_ref,
    query_ref,
    prior_ref,
    own_ref,
    row_request_ref,
    row_id_ref,
    key_request_ref,
    key_id_ref,
    rank_ref,
    *refs,
):
    shard_refs = refs[:shards]
    out_refs = refs[shards : shards + slots]
    routes_ref, pool_ref, peak_ref, total_ref, sum_ref, arrived, told = refs[shards + slots :]
    me = scalar_ref[0]
    in_first = scalar_ref[1]
    rows = query_ref.shape[2]
    blocks = rows // BLOCK
    shard_rows = shard_refs[0].shape[0] - TAIL
    shard_pages = shard_rows // PAGE

    for d in range(shards):
        def start(j, carry, d=d):
            page = (me ^ d) * shard_pages + j
            pltpu.make_async_copy(
                shard_refs[d].at[pl.ds(pl.multiple_of(j * PAGE, PAGE), PAGE), :],
                pool_ref.at[pl.ds(pl.multiple_of(place_ref[page] * PAGE, PAGE), PAGE), :],
                arrived,
            ).start()
            return carry

        lax.fori_loop(0, shard_pages, start, 0)
        pltpu.make_async_copy(
            shard_refs[d].at[shard_rows : shard_rows + TAIL, : routes_ref.shape[1]],
            routes_ref.at[d * TAIL : (d + 1) * TAIL, :],
            told,
        ).start()

    def near(b, carry):
        at = pl.ds(pl.multiple_of(b * BLOCK, BLOCK), BLOCK)
        request = row_request_ref[at, :]
        ident = row_id_ref[at, :]
        allowed = (key_request_ref[...] == request) & (key_id_ref[...] <= ident)
        allowed = jnp.concatenate([allowed.astype(jnp.float32)] * QPG, axis=0) > 0.0
        for j in range(kv_dev):
            queries = query_ref[j, :, at, :].reshape(QPG * BLOCK, LANES)
            columns = slice(j * LANES, (j + 1) * LANES)
            keys = jnp.concatenate([prior_ref[:, columns], own_ref[:, columns]], axis=0)
            scores = jnp.where(allowed, scored(queries, keys), MASKED)
            peak = jnp.max(scores, axis=-1, keepdims=True)
            weights = jnp.where(allowed, jnp.exp(scores - peak), 0.0)
            total = jnp.sum(weights, axis=-1, keepdims=True)
            mixed = jnp.dot(
                weights.astype(jnp.bfloat16), keys, preferred_element_type=jnp.float32
            )
            shape = (QPG, BLOCK, LANES)
            peak_ref[j, :, at, :] = jnp.broadcast_to(peak, mixed.shape).reshape(shape)
            total_ref[j, :, at, :] = jnp.broadcast_to(total, mixed.shape).reshape(shape)
            sum_ref[j, :, at, :] = mixed.reshape(shape)
        return carry

    lax.fori_loop(0, blocks, near, 0)
    pltpu.make_async_copy(pool_ref, pool_ref, arrived).wait()
    pltpu.make_async_copy(routes_ref, routes_ref, told).wait()

    group_rows = pool_ref.shape[0] // GROUPS
    full = (in_first + BLOCK - 1) // BLOCK
    skip = in_first // BLOCK

    def far(item, carry):
        group = (item >= full).astype(jnp.int32)
        b = jnp.where(item < full, item, item - full + skip)
        at = pl.ds(pl.multiple_of(b * BLOCK, BLOCK), BLOCK)
        keys_at = pl.ds(pl.multiple_of(group * group_rows, group_rows), group_rows)
        line = lax.broadcasted_iota(jnp.int32, (QPG, BLOCK, LANES), 1) + b * BLOCK
        chosen = (line >= in_first) == (group == 1)
        shape = (QPG, BLOCK, LANES)
        for j in range(kv_dev):
            queries = query_ref[j, :, at, :].reshape(QPG * BLOCK, LANES)
            keys = pool_ref[keys_at, j * LANES : (j + 1) * LANES]
            scores = scored(queries, keys)
            here = jnp.max(scores, axis=-1, keepdims=True)
            weights = jnp.exp(scores - here)
            total = jnp.sum(weights, axis=-1, keepdims=True)
            mixed = jnp.dot(
                weights.astype(jnp.bfloat16), keys, preferred_element_type=jnp.float32
            ).reshape(shape)
            here = jnp.broadcast_to(here, (QPG * BLOCK, LANES)).reshape(shape)
            total = jnp.broadcast_to(total, (QPG * BLOCK, LANES)).reshape(shape)
            before = peak_ref[j, :, at, :]
            peak = jnp.maximum(before, here)
            keep, gain = jnp.exp(before - peak), jnp.exp(here - peak)
            joint_total = total_ref[j, :, at, :] * keep + total * gain
            joint_sum = sum_ref[j, :, at, :] * keep + mixed * gain
            total_ref[j, :, at, :] = jnp.where(chosen, joint_total, total_ref[j, :, at, :])
            sum_ref[j, :, at, :] = jnp.where(chosen, joint_sum, sum_ref[j, :, at, :])
        return carry

    lax.fori_loop(0, full + blocks - skip, far, 0)

    back = (rank_ref[...] == lax.broadcasted_iota(jnp.int32, (rows, rows), 1)).astype(jnp.bfloat16)
    lane = lax.broadcasted_iota(jnp.int32, (rows, LANES), 1)
    piece = rows // slots
    heads = [
        sum_ref[j, i] / total_ref[j, i] for j in range(kv_dev) for i in range(QPG)
    ]
    for h in range(0, len(heads), 2):
        pair = pltpu.roll(heads[h], HD, 1)
        if h + 1 < len(heads):
            pair = jnp.where(lane < HD, pair, heads[h + 1])
        pair = jnp.dot(
            back, pair.astype(jnp.bfloat16), preferred_element_type=jnp.float32
        ).astype(jnp.bfloat16)
        width = min(LANES, len(heads) * HD - h * HD)
        for k in range(slots):
            out_refs[k][:, h * HD : h * HD + width] = pair[k * piece : (k + 1) * piece, :width]


def close_kernel(slots, scalar_ref, hidden_ref, weight_ref, gain_ref, *refs):
    context_refs = refs[:slots]
    branch_ref, mid_ref, mixed_ref = refs[slots:]
    width = context_refs[0].shape[1]
    total = None
    for k in range(slots):
        first = pl.multiple_of((scalar_ref[0] ^ k) * width, width)
        part = jnp.dot(
            context_refs[k][...],
            weight_ref[pl.ds(first, width), :],
            preferred_element_type=jnp.float32,
        )
        total = part if total is None else total + part
    branch = total.astype(jnp.bfloat16)
    branch_ref[...] = branch
    mid = (hidden_ref[...].astype(jnp.float32) + branch.astype(jnp.float32)).astype(jnp.bfloat16)
    mid_ref[...] = mid
    wide = mid.astype(jnp.float32)
    scale = lax.rsqrt(jnp.mean(wide * wide, axis=-1, keepdims=True) + EPSILON)
    mixed_ref[...] = (wide * scale * gain_ref[...]).astype(jnp.bfloat16)


def expert_kernel(offsets, parts, where_ref, *refs):
    count = len(offsets)
    state_refs = refs[:count]
    routes_ref, router_ref, up_ref, down_ref = refs[count : count + 4]
    swapped = refs[count + 4 : count + 4 + 3 * parts]
    out_refs = refs[count + 4 + 3 * parts :]
    rows = state_refs[0].shape[0]
    lanes = router_ref.shape[1]
    experts_here = up_ref.shape[0]
    states = jnp.concatenate([ref[...] for ref in state_refs], axis=0)
    lane = lax.broadcasted_iota(jnp.int32, (rows, lanes), 1)
    hits = []
    for d in offsets:
        routes = routes_ref[d * TAIL : (d + 1) * TAIL, :].astype(jnp.float32)
        routes = jnp.transpose(routes).astype(jnp.int32)
        hit = jnp.zeros((rows, lanes), jnp.float32)
        for k in range(TOPK):
            hit = jnp.where(lane == routes[:, k : k + 1], 1.0, hit)
        hits.append(hit)
    hit = jnp.concatenate(hits, axis=0) > 0.0
    logits = jnp.dot(states, router_ref[...], preferred_element_type=jnp.float32)
    logits = jnp.where(hit, logits, MASKED)
    peak = jnp.max(logits, axis=-1, keepdims=True)
    shares = jnp.where(hit, jnp.exp(logits - peak), 0.0)
    shares = shares / jnp.sum(shares, axis=-1, keepdims=True)
    lane = lax.broadcasted_iota(jnp.int32, shares.shape, 1)

    def gate_of(expert):
        return jnp.sum(jnp.where(lane == expert, shares, 0.0), axis=-1, keepdims=True)

    def through(lead, rest, down):
        activated = (lead / (1.0 + jnp.exp(-lead)) * rest).astype(jnp.bfloat16)
        return jnp.dot(activated, down, preferred_element_type=jnp.float32)

    result = None
    for x in range(experts_here):
        joined = jnp.dot(states, up_ref[x], preferred_element_type=jnp.float32)
        part = through(joined[:, :FFE], joined[:, FFE:], down_ref[x])
        part = gate_of(where_ref[0] * experts_here + x) * part
        result = part if result is None else result + part
    for x in range(experts_here):
        total = None
        for k in range(parts):
            lead_ref, rest_ref, other_ref = swapped[3 * k : 3 * k + 3]
            lead = jnp.dot(states, lead_ref[x], preferred_element_type=jnp.float32)
            rest = jnp.dot(states, rest_ref[x], preferred_element_type=jnp.float32)
            part = through(lead, rest, other_ref[x])
            total = part if total is None else total + part
        result = result + gate_of(where_ref[1] * experts_here + x) * total
    for i in range(count):
        out_refs[i][...] = result[i * rows : (i + 1) * rows].astype(jnp.bfloat16)


def run_experts(slots, offsets, where, routes, router, w_gate_up, w_down, swapped):
    count = len(offsets)
    outs = pl.pallas_call(
        functools.partial(expert_kernel, offsets, len(swapped) // 3),
        out_shape=[jax.ShapeDtypeStruct(slots[d].shape, jnp.bfloat16) for d in offsets],
        in_specs=[SMEM] + [VMEM] * (count + 4 + len(swapped)),
        out_specs=[VMEM] * count,
        compiler_params=params(28),
        name="experts",
    )(where, *[slots[d] for d in offsets], routes, router, w_gate_up, w_down, *swapped)
    return dict(zip(offsets, outs))


def per_device(
    hidden,
    attn_gain,
    w_qkv,
    kv_cache,
    page_table,
    lengths,
    request_group,
    key_mask,
    o_weight,
    moe_gain,
    router,
    routes,
    w_gate_up,
    w_down,
):
    n_tok = lax.axis_size("tok")
    n_head = lax.axis_size("head")
    tok_dev = hidden.shape[0]
    row_tokens = tok_dev * n_head
    kv_dev = w_qkv.shape[1] // ((QPG + 2) * HD)
    row_index = lax.axis_index("tok")
    head_index = lax.axis_index("head")

    states = spread(hidden, "head", bits_of(n_head))
    told = jnp.pad(
        routes.T.astype(jnp.bfloat16),
        ((0, TAIL - TOPK), (0, kv_cache.shape[1] - tok_dev)),
    )
    swap = min(2, n_tok // 2)
    shards = spread(jnp.concatenate([kv_cache, told], axis=0), "tok", bits_of(n_tok))

    share = FFE // n_head
    lead = lax.dynamic_slice_in_dim(w_gate_up, head_index * share, share, 2)
    rest = lax.dynamic_slice_in_dim(w_gate_up, FFE + head_index * share, share, 2)
    down = lax.dynamic_slice_in_dim(w_down, head_index * share, share, 1)
    lead, rest, down, _ = lax.optimization_barrier(
        (lead, rest, down, shards[n_tok - 1 - (swap - 1)])
    )
    triple = [
        spread(crossed(w, "tok", swap), "head", bits_of(n_head)) for w in (lead, rest, down)
    ]
    swapped = [w[k] for k in range(n_head) for w in triple]

    within = jnp.arange(tok_dev, dtype=jnp.int32)
    row_offset = jnp.concatenate(
        [(head_index ^ k).astype(jnp.int32) * tok_dev + within for k in range(n_head)]
    )
    own_ids = row_index * row_tokens + row_offset
    prior_ids = own_ids - row_tokens
    own_request, own_start, own_group = token_info(own_ids, lengths, request_group)
    prior_request, _, prior_group = token_info(prior_ids, lengths, request_group)
    rank, in_first = ranks(own_group)
    prior_rank, _ = ranks(prior_group)
    token_mask = jnp.concatenate([jnp.zeros((row_tokens,), jnp.int32), key_mask])
    window = lax.dynamic_slice_in_dim(token_mask, row_index * row_tokens, 2 * row_tokens)
    window = window.reshape(2 * n_head, tok_dev)
    flipped = [(head_index ^ k) for k in range(n_head)]
    prior_mask = jnp.concatenate([window[f] for f in flipped])
    own_mask = jnp.concatenate([window[n_head + f] for f in flipped])
    ids = arranged(own_ids, rank)
    request = arranged(own_request, rank)
    position = (PREFIX + arranged(own_ids - own_start, rank)).astype(jnp.float32)
    key_request = jnp.concatenate(
        [
            arranged(jnp.where(prior_mask == 1, prior_request, -1), prior_rank),
            arranged(jnp.where(own_mask == 1, own_request, -1), rank),
        ]
    )
    key_ids = jnp.concatenate([arranged(prior_ids, prior_rank), ids])
    half = HD // 2
    inv_freq = ROPE_BASE ** (-2.0 * jnp.arange(half, dtype=jnp.float32) / HD)
    angles = position[:, None] * jnp.tile(inv_freq, LANES // half)[None, :]
    sign = jnp.where(jnp.arange(LANES, dtype=jnp.int32) % HD < half, -1.0, 1.0)
    cosine = jnp.cos(angles)
    sine = jnp.sin(angles) * sign[None, :]
    n_pages = page_table.shape[0]
    pages = jnp.arange(n_pages, dtype=jnp.int32)
    place = jnp.sum(
        jnp.where(page_table[:, None] == pages[None, :], pages[:, None], 0), axis=0
    )
    experts = router.shape[1]
    wide_router = jnp.pad(router, ((0, 0), (0, -experts % LANES)))
    place, key_request, key_ids, wide_router, cosine, sine = lax.optimization_barrier(
        (place, key_request, key_ids, wide_router, cosine, sine)
    )

    columns = w_qkv.shape[1]
    queries, own_kv = pl.pallas_call(
        functools.partial(project_kernel, n_head, kv_dev),
        out_shape=[
            jax.ShapeDtypeStruct((kv_dev, QPG, row_tokens, LANES), jnp.bfloat16),
            jax.ShapeDtypeStruct((row_tokens, kv_dev * LANES), jnp.bfloat16),
        ],
        in_specs=[VMEM] * (5 + n_head),
        out_specs=[VMEM] * 2,
        compiler_params=params(36),
        name="project",
    )(
        rank[None, :],
        attn_gain[None, :],
        jnp.pad(w_qkv, ((0, 0), (0, -columns % LANES))),
        cosine,
        sine,
        *[states[k] for k in range(n_head)],
    )
    prior_kv = lax.ppermute(own_kv, "tok", [(i, i + 1) for i in range(n_tok - 1)])
    pool_rows = kv_cache.shape[0] * n_tok
    *contexts, all_routes = pl.pallas_call(
        functools.partial(attend_kernel, n_tok, kv_dev, n_head),
        out_shape=[jax.ShapeDtypeStruct((tok_dev, kv_dev * QPG * HD), jnp.bfloat16)] * n_head
        + [jax.ShapeDtypeStruct((n_tok * TAIL, tok_dev), jnp.bfloat16)],
        in_specs=[SMEM] * 2 + [VMEM] * 8 + [pl.BlockSpec(memory_space=pl.ANY)] * n_tok,
        out_specs=[VMEM] * (n_head + 1),
        scratch_shapes=[pltpu.VMEM((pool_rows, kv_cache.shape[1]), jnp.bfloat16)]
        + [pltpu.VMEM((kv_dev, QPG, row_tokens, LANES), jnp.float32)] * 3
        + [pltpu.SemaphoreType.DMA] * 2,
        compiler_params=params(36),
        name="attend",
    )(
        jnp.stack([row_index, in_first]).astype(jnp.int32),
        place,
        queries,
        prior_kv,
        own_kv,
        request[:, None],
        ids[:, None],
        key_request[None, :],
        key_ids[None, :],
        rank[:, None],
        *[shards[d] for d in range(n_tok)],
    )
    context_slots = [contexts[0]] + [crossed(contexts[k], "head", k) for k in range(1, n_head)]
    attn_sum, mid_states, mixed = pl.pallas_call(
        functools.partial(close_kernel, n_head),
        out_shape=[jax.ShapeDtypeStruct(hidden.shape, jnp.bfloat16)] * 3,
        in_specs=[SMEM] + [VMEM] * (3 + n_head),
        out_specs=[VMEM] * 3,
        compiler_params=params(20),
        name="close",
    )(
        head_index.astype(jnp.int32)[None],
        hidden,
        o_weight,
        moe_gain[None, :],
        *context_slots,
    )

    walk = [bit for bit in bits_of(n_tok) if bit != swap]
    slots = spread(mixed, "tok", walk)
    order = sorted(slots)
    where = jnp.stack([row_index, row_index ^ swap]).astype(jnp.int32)
    wide_router, w_gate_up, w_down, *swapped = [
        pinned(w) for w in (wide_router, w_gate_up, w_down, *swapped)
    ]
    parts = {}
    for first in range(0, len(order), 2):
        parts.update(
            run_experts(
                slots,
                order[first : first + 2],
                where,
                all_routes,
                wide_router,
                w_gate_up,
                w_down,
                swapped,
            )
        )
    routed_sum = folded(parts, "tok", walk[::-1]).astype(jnp.float32)
    layer_out = (mid_states.astype(jnp.float32) + routed_sum).astype(jnp.bfloat16)
    return (attn_sum, layer_out)


def solution(mesh):
    return jax.shard_map(
        per_device,
        mesh=mesh,
        in_specs=(
            P(("tok", "head"), None),
            P(),
            P(None, "head"),
            P("tok", "head"),
            P(),
            P(),
            P(),
            P(),
            P(),
            P(),
            P(),
            P(("tok", "head"), None),
            P("tok", None, None),
            P("tok", None, None),
        ),
        out_specs=(P(("tok", "head"), None), P(("tok", "head"), None)),
        check_vma=False,
    )
```

```python
import functools

import jax
import jax.numpy as jnp
import numpy as np
from jax import lax
from jax.experimental import pallas as pl
from jax.experimental.pallas import tpu as pltpu
from jax.sharding import PartitionSpec as P

D = 1536
HEADS = 24
KVH = 8
HD = 64
FFE = 512
TOPK = 8
PREFIX = 2048
GROUPS = 2
PAGE = 16
QPG = HEADS // KVH
BLOCK = 64


EPSILON = 1e-06
ROPE_BASE = 10000.0
MASKED = -1e30

LANES = 128


def crossed(array, axis, flip):
    count = lax.axis_size(axis)
    return lax.ppermute(array, axis, [(i, i ^ flip) for i in range(count)])


def spread(own, axis, bits):
    slots = {0: own}
    for bit in bits:
        for d in sorted(slots):
            slots[d | bit] = crossed(slots[d], axis, bit)
    return slots


def spread_by_stages(own, axis, bits, also):
    slots = {0: own}
    for stage in range(1, len(bits) + 1):
        coming = {}
        for d in slots:
            low = [bit for bit in bits if bit & d]
            for bit in bits[bits.index(low[-1]) + 1 if low else 0 :]:
                if bin(d).count("1") == stage - 1:
                    coming[d | bit] = crossed(slots[d], axis, bit)
        names = sorted(coming)
        came = lax.optimization_barrier([coming[d] for d in names] + (also if stage == 1 else []))
        slots.update(zip(names, came))
        also = came[len(names) :] if stage == 1 else also
    return slots, also


def folded(parts, axis, bits):
    parts = dict(parts)
    for bit in bits:
        for d in sorted(parts, reverse=True):
            if d & bit:
                came = crossed(parts.pop(d).astype(jnp.bfloat16), axis, bit)
                parts[d ^ bit] = parts[d ^ bit].astype(jnp.float32) + came.astype(jnp.float32)
    return parts[0]


def bits_of(count):
    return [1 << i for i in reversed(range(count.bit_length() - 1))]


VMEM = pl.BlockSpec(memory_space=pltpu.VMEM)
SMEM = pl.BlockSpec(memory_space=pltpu.SMEM)
TAIL = 16
ATT = 16


def params(mib):
    return pltpu.CompilerParams(vmem_limit_bytes=mib << 20)


def spent(flops):
    return pl.CostEstimate(flops=flops, transcendentals=0, bytes_accessed=0)


def pinned(array):
    return pltpu.with_memory_space_constraint(array, pltpu.VMEM)


def project_kernel(
    slots,
    kv_dev,
    where_ref,
    requests_ref,
    mask_ref,
    frequency_ref,
    gain_ref,
    weight_ref,
    *refs,
):
    state_refs = refs[:slots]
    query_ref, kv_ref, column_ref, row_ref, first_ref = refs[slots:]
    row_index, head_index = where_ref[0], where_ref[1]
    piece = state_refs[0].shape[0]
    rows = piece * slots
    real = jnp.float32
    rounded = jnp.bfloat16

    table = requests_ref[...]
    turned_table = jnp.transpose(table)
    width = table.shape[1]
    across = lax.broadcasted_iota(jnp.int32, (width, width), 1)
    along = lax.broadcasted_iota(jnp.int32, (width, width), 0)
    ends = jnp.sum(jnp.where(along <= across, turned_table[:, 0:1], 0.0), axis=0, keepdims=True)
    ends_up = jnp.sum(jnp.where(across <= along, table[0:1], 0.0), axis=1, keepdims=True)
    starts, starts_up = ends - table[0:1], ends_up - turned_table[:, 0:1]

    def offsets(shape, axis):
        place = lax.broadcasted_iota(jnp.int32, shape, axis)
        shift = jnp.zeros(shape, jnp.int32)
        for k in range(slots):
            shift = jnp.where(place // piece == k, ((head_index ^ k) - k) * piece, shift)
        return place + shift

    local, local_up = offsets((1, rows), 1), offsets((rows, 1), 0)
    across = lax.broadcasted_iota(jnp.int32, (rows, rows), 1).astype(real)
    along = lax.broadcasted_iota(jnp.int32, (rows, rows), 0).astype(real)
    lane = lax.broadcasted_iota(jnp.int32, (rows, LANES), 1)

    def tables(behind):
        first = (row_index - behind) * rows
        ids, ids_up = (local + first).astype(real), (local_up + first).astype(real)
        holds = (starts_up <= ids) & (ids < ends_up)
        holds_up = (starts <= ids_up) & (ids_up < ends)
        number = lax.broadcasted_iota(jnp.int32, (width, 1), 0).astype(real)
        request = jnp.sum(jnp.where(holds, number, 0.0), axis=0, keepdims=True)
        start = jnp.sum(jnp.where(holds, starts_up, 0.0), axis=0, keepdims=True)
        group = jnp.sum(jnp.where(holds, turned_table[:, 1:2], 0.0), axis=0, keepdims=True)
        group_up = jnp.sum(jnp.where(holds_up, table[1:2], 0.0), axis=1, keepdims=True)
        key = group * (2.0 * rows) + lax.broadcasted_iota(jnp.int32, (1, rows), 1).astype(real)
        key_up = group_up * (2.0 * rows) + lax.broadcasted_iota(jnp.int32, (rows, 1), 0).astype(real)
        rank = jnp.sum(jnp.where(key_up < key, 1.0, 0.0), axis=0, keepdims=True)
        rank_up = jnp.sum(jnp.where(key < key_up, 1.0, 0.0), axis=1, keepdims=True)
        place = rank == along

        def arranged(values):
            return jnp.sum(jnp.where(place, values, 0.0), axis=1, keepdims=True)

        marks = []
        for k in range(slots):
            block = (row_index - behind) * slots + (head_index ^ k)
            mark = mask_ref[pl.ds(jnp.maximum(block, 0), 1), :]
            marks.append(jnp.where(block >= 0, mark, 0))
        mark = jnp.concatenate(marks, axis=1)
        open_request = arranged(jnp.where(mark == 1, request, -1.0))
        ids = arranged(ids)
        columns = jnp.where(lane == 0, open_request, jnp.where(lane == 1, ids, 0.0))
        return columns, ids, arranged(request), arranged(start), place, rank_up, group

    before = tables(1)[0]
    columns, ids, request, start, place, rank_up, group = tables(0)
    columns = jnp.where(lane == 2, request, jnp.where(lane == 3, rank_up, columns))
    column_ref[...] = columns
    row_ref[:, :rows] = jnp.transpose(before)[:8]
    row_ref[:, rows:] = jnp.transpose(columns)[:8]
    first_ref[0] = jnp.sum(jnp.where(group == 0.0, 1.0, 0.0)).astype(jnp.int32)
    angles = (PREFIX + ids - start) * frequency_ref[...]
    cosine = jnp.cos(angles)
    sine = jnp.where(lane % HD < HD // 2, -1.0, 1.0) * jnp.sin(angles)

    states = jnp.concatenate([ref[...] for ref in state_refs], axis=0).astype(real)
    scale = lax.rsqrt(jnp.mean(states * states, axis=-1, keepdims=True) + EPSILON)
    normed = (states * scale * gain_ref[...]).astype(rounded)
    chosen = jnp.where(place, 1.0, 0.0).astype(rounded)
    normed = jnp.dot(chosen, normed, preferred_element_type=real).astype(rounded)
    projected = jnp.dot(normed, weight_ref[...], preferred_element_type=real)
    low = lane < HD
    first = lane % HD < HD // 2

    def tile(number):
        return projected[:, number * LANES : (number + 1) * LANES]

    @functools.cache
    def turned(number):
        plain = tile(number)
        partner = jnp.where(
            first, pltpu.roll(plain, LANES - HD // 2, 1), pltpu.roll(plain, HD // 2, 1)
        )
        return plain * cosine + partner * sine

    for j in range(kv_dev):
        unit = j * (QPG + 2)
        for i in range(QPG):
            query = turned((unit + i) // 2)
            if (unit + i) % 2:
                query = pltpu.roll(query, HD, 1)
            query_ref[j, i] = jnp.where(low, query * HD ** (-0.5), 0.0).astype(rounded)
        key, value = turned((unit + QPG) // 2), tile((unit + QPG + 1) // 2)
        if (unit + QPG) % 2:
            key, value = pltpu.roll(key, HD, 1), pltpu.roll(value, HD, 1)
        kv_ref[:, j * LANES : (j + 1) * LANES] = jnp.where(low, key, value).astype(rounded)


def scored(queries, keys):
    return lax.dot_general(
        queries, keys, (((1,), (1,)), ((), ())), preferred_element_type=jnp.float32
    )


def attend_kernel(
    shards,
    heads_at,
    slots,
    scalar_ref,
    first_ref,
    place_ref,
    query_ref,
    prior_ref,
    own_ref,
    column_ref,
    row_ref,
    *refs,
):
    shard_refs = refs[:shards]
    out_refs = refs[shards : shards + slots]
    routes_ref, pool_ref, peak_ref, total_ref, sum_ref, arrived, told = refs[shards + slots :]
    me = scalar_ref[0]
    in_first = first_ref[0]
    first_head, kv_dev = heads_at
    mine = slice(first_head * LANES, (first_head + kv_dev) * LANES)
    rows = query_ref.shape[2]
    blocks = rows // BLOCK
    shard_rows = shard_refs[0].shape[0] - TAIL
    shard_pages = shard_rows // PAGE

    for d in range(shards):
        def start(j, carry, d=d):
            page = (me ^ d) * shard_pages + j
            pltpu.make_async_copy(
                shard_refs[d].at[pl.ds(pl.multiple_of(j * PAGE, PAGE), PAGE), mine],
                pool_ref.at[pl.ds(pl.multiple_of(place_ref[page] * PAGE, PAGE), PAGE), :],
                arrived,
            ).start()
            return carry

        lax.fori_loop(0, shard_pages, start, 0, unroll=True)
        pltpu.make_async_copy(
            shard_refs[d].at[shard_rows : shard_rows + TAIL, : routes_ref.shape[1]],
            routes_ref.at[d * TAIL : (d + 1) * TAIL, :],
            told,
        ).start()

    def near(b, carry):
        at = pl.ds(pl.multiple_of(b * BLOCK, BLOCK), BLOCK)
        column = column_ref[at, :]
        row = row_ref[...]
        allowed = (row[0:1] == column[:, 2:3]) & (row[1:2] <= column[:, 1:2])
        allowed = jnp.concatenate([allowed.astype(jnp.float32)] * QPG, axis=0) > 0.0
        for j in range(kv_dev):
            queries = query_ref[first_head + j, :, at, :].reshape(QPG * BLOCK, LANES)
            columns = slice((first_head + j) * LANES, (first_head + j + 1) * LANES)
            keys = jnp.concatenate([prior_ref[:, columns], own_ref[:, columns]], axis=0)
            scores = jnp.where(allowed, scored(queries, keys), MASKED)
            peak = jnp.max(scores, axis=-1, keepdims=True)
            weights = jnp.where(allowed, jnp.exp(scores - peak), 0.0)
            total = jnp.sum(weights, axis=-1, keepdims=True)
            mixed = jnp.dot(
                weights.astype(jnp.bfloat16), keys, preferred_element_type=jnp.float32
            )
            shape = (QPG, BLOCK, LANES)
            peak_ref[j, :, at, :] = jnp.broadcast_to(peak, mixed.shape).reshape(shape)
            total_ref[j, :, at, :] = jnp.broadcast_to(total, mixed.shape).reshape(shape)
            sum_ref[j, :, at, :] = mixed.reshape(shape)
        return carry

    lax.fori_loop(0, blocks, near, 0)
    pltpu.make_async_copy(pool_ref, pool_ref, arrived).wait()
    pltpu.make_async_copy(routes_ref, routes_ref, told).wait()

    group_rows = pool_ref.shape[0] // GROUPS
    full = (in_first + BLOCK - 1) // BLOCK
    skip = in_first // BLOCK

    def far(item, carry):
        group = (item >= full).astype(jnp.int32)
        b = jnp.where(item < full, item, item - full + skip)
        at = pl.ds(pl.multiple_of(b * BLOCK, BLOCK), BLOCK)
        keys_at = pl.ds(pl.multiple_of(group * group_rows, group_rows), group_rows)
        line = lax.broadcasted_iota(jnp.int32, (QPG, BLOCK, LANES), 1) + b * BLOCK
        chosen = (line >= in_first) == (group == 1)
        shape = (QPG, BLOCK, LANES)
        for j in range(kv_dev):
            queries = query_ref[first_head + j, :, at, :].reshape(QPG * BLOCK, LANES)
            keys = pool_ref[keys_at, j * LANES : (j + 1) * LANES]
            scores = scored(queries, keys)
            here = jnp.max(scores, axis=-1, keepdims=True)
            weights = jnp.exp(scores - here)
            total = jnp.sum(weights, axis=-1, keepdims=True)
            mixed = jnp.dot(
                weights.astype(jnp.bfloat16), keys, preferred_element_type=jnp.float32
            ).reshape(shape)
            here = jnp.broadcast_to(here, (QPG * BLOCK, LANES)).reshape(shape)
            total = jnp.broadcast_to(total, (QPG * BLOCK, LANES)).reshape(shape)
            before = peak_ref[j, :, at, :]
            peak = jnp.maximum(before, here)
            keep, gain = jnp.exp(before - peak), jnp.exp(here - peak)
            joint_total = total_ref[j, :, at, :] * keep + total * gain
            joint_sum = sum_ref[j, :, at, :] * keep + mixed * gain
            total_ref[j, :, at, :] = jnp.where(chosen, joint_total, total_ref[j, :, at, :])
            sum_ref[j, :, at, :] = jnp.where(chosen, joint_sum, sum_ref[j, :, at, :])
        return carry

    lax.fori_loop(0, full + blocks - skip, far, 0)

    place = lax.broadcasted_iota(jnp.int32, (rows, rows), 1).astype(jnp.float32)
    back = jnp.where(column_ref[...][:, 3:4] == place, 1.0, 0.0).astype(jnp.bfloat16)
    lane = lax.broadcasted_iota(jnp.int32, (rows, LANES), 1)
    piece = rows // slots
    heads = [
        sum_ref[j, i] / total_ref[j, i] for j in range(kv_dev) for i in range(QPG)
    ]
    for h in range(0, len(heads), 2):
        pair = pltpu.roll(heads[h], HD, 1)
        if h + 1 < len(heads):
            pair = jnp.where(lane < HD, pair, heads[h + 1])
        pair = jnp.dot(
            back, pair.astype(jnp.bfloat16), preferred_element_type=jnp.float32
        ).astype(jnp.bfloat16)
        width = min(LANES, len(heads) * HD - h * HD)
        for k in range(slots):
            out_refs[k][:, h * HD : h * HD + width] = pair[k * piece : (k + 1) * piece, :width]


def close_kernel(slots, scalar_ref, hidden_ref, weight_ref, gain_ref, *refs):
    branch_ref, mid_ref, mixed_ref = refs[-3:]
    context_refs = refs[:-3]
    pieces = len(context_refs) // slots
    head_width = sum(ref.shape[1] for ref in context_refs[:pieces])
    total = None
    for k in range(slots):
        first = (scalar_ref[1] ^ k) * head_width
        for ref in context_refs[k * pieces : (k + 1) * pieces]:
            width = ref.shape[1]
            part = jnp.dot(
                ref[...],
                weight_ref[pl.ds(pl.multiple_of(first, HD), width), :],
                preferred_element_type=jnp.float32,
            )
            first = first + width
            total = part if total is None else total + part
    branch = total.astype(jnp.bfloat16)
    branch_ref[...] = branch
    mid = (hidden_ref[...].astype(jnp.float32) + branch.astype(jnp.float32)).astype(jnp.bfloat16)
    mid_ref[...] = mid
    wide = mid.astype(jnp.float32)
    scale = lax.rsqrt(jnp.mean(wide * wide, axis=-1, keepdims=True) + EPSILON)
    mixed_ref[...] = (wide * scale * gain_ref[...]).astype(jnp.bfloat16)


def expert_kernel(offsets, swap, parts, where_ref, *refs):
    count = len(offsets)
    state_refs = refs[:count]
    routes_ref, router_ref, up_ref, down_ref = refs[count : count + 4]
    swapped = refs[count + 4 : count + 4 + 2 * parts]
    other_ref = refs[count + 4 + 2 * parts]
    out_refs = refs[count + 5 + 2 * parts :]
    rows = state_refs[0].shape[0]
    lanes = router_ref.shape[0]
    experts_here = up_ref.shape[0]
    states = jnp.concatenate([ref[...] for ref in state_refs], axis=0)
    lane = lax.broadcasted_iota(jnp.int32, (rows, lanes), 1)
    hits = []
    for d in offsets:
        routes = routes_ref[d * TAIL : (d + 1) * TAIL, :].astype(jnp.float32)
        routes = jnp.transpose(routes).astype(jnp.int32)
        hit = jnp.zeros((rows, lanes), jnp.float32)
        for k in range(TOPK):
            hit = jnp.where(lane == routes[:, k : k + 1], 1.0, hit)
        hits.append(hit)
    hit = jnp.concatenate(hits, axis=0) > 0.0
    logits = scored(states, router_ref[...])
    logits = jnp.where(hit, logits, MASKED)
    peak = jnp.max(logits, axis=-1, keepdims=True)
    shares = jnp.where(hit, jnp.exp(logits - peak), 0.0)
    shares = shares / jnp.sum(shares, axis=-1, keepdims=True)
    lane = lax.broadcasted_iota(jnp.int32, shares.shape, 1)

    def gate_of(expert):
        return jnp.sum(jnp.where(lane == expert, shares, 0.0), axis=-1, keepdims=True)

    def through(lead, rest, down):
        activated = (lead / (1.0 + jnp.exp(-lead)) * rest).astype(jnp.bfloat16)
        return jnp.dot(activated, down, preferred_element_type=jnp.float32)

    result = None
    for x in range(experts_here):
        joined = jnp.dot(states, up_ref[x], preferred_element_type=jnp.float32)
        part = through(joined[:, :FFE], joined[:, FFE:], down_ref[x])
        part = gate_of(where_ref[0] * experts_here + x) * part
        result = part if result is None else result + part
    for x in range(experts_here):
        total = None
        for k in range(parts):
            lead_ref, rest_ref = swapped[2 * k : 2 * k + 2]
            share = lead_ref.shape[2]
            first = pl.multiple_of((where_ref[1] ^ k) * share, share)
            lead = jnp.dot(states, lead_ref[x], preferred_element_type=jnp.float32)
            rest = jnp.dot(states, rest_ref[x], preferred_element_type=jnp.float32)
            part = through(lead, rest, other_ref[x, pl.ds(first, share), :])
            total = part if total is None else total + part
        result = result + gate_of((where_ref[0] ^ swap) * experts_here + x) * total
    for i in range(count):
        out_refs[i][...] = result[i * rows : (i + 1) * rows].astype(jnp.bfloat16)


def run_experts(slots, offsets, where, swap, routes, router, w_gate_up, w_down, swapped):
    count = len(offsets)
    outs = pl.pallas_call(
        functools.partial(expert_kernel, offsets, swap, len(swapped) // 2),
        out_shape=[jax.ShapeDtypeStruct(slots[d].shape, jnp.bfloat16) for d in offsets],
        in_specs=[SMEM] + [VMEM] * (count + 4 + len(swapped)),
        out_specs=[VMEM] * count,
        compiler_params=params(28),
        cost_estimate=spent(count * 128 * D * FFE * 6 * 4),
        name="experts",
    )(where, *[slots[d] for d in offsets], routes, router, w_gate_up, w_down, *swapped)
    return dict(zip(offsets, outs))


def share_kernel(where_ref, up_ref, lead_ref, rest_ref, done):
    share = lead_ref.shape[2]
    at = pl.multiple_of(where_ref[1] * share, share)
    copies = [
        pltpu.make_async_copy(up_ref.at[:, :, pl.ds(at, share)], lead_ref, done.at[0]),
        pltpu.make_async_copy(up_ref.at[:, :, pl.ds(FFE + at, share)], rest_ref, done.at[1]),
    ]
    for copy in copies:
        copy.start()
    for copy in copies:
        copy.wait()


def shares_of(place_here, n_head, w_gate_up):
    share = FFE // n_head
    if share % LANES:
        first = place_here[1] * share
        return (
            lax.dynamic_slice_in_dim(w_gate_up, first, share, 2),
            lax.dynamic_slice_in_dim(w_gate_up, FFE + first, share, 2),
        )
    whole = pl.BlockSpec(memory_space=pltpu.HBM)
    return pl.pallas_call(
        share_kernel,
        out_shape=[pltpu.HBM((w_gate_up.shape[0], D, share), jnp.bfloat16)] * 2,
        in_specs=[SMEM, whole],
        out_specs=[whole] * 2,
        scratch_shapes=[pltpu.SemaphoreType.DMA((2,))],
        compiler_params=params(2),
        name="shares",
    )(place_here, w_gate_up)


def per_device(
    hidden,
    attn_gain,
    w_qkv,
    kv_cache,
    page_table,
    lengths,
    request_group,
    key_mask,
    o_weight,
    moe_gain,
    router,
    routes,
    w_gate_up,
    w_down,
):
    n_tok = lax.axis_size("tok")
    n_head = lax.axis_size("head")
    tok_dev = hidden.shape[0]
    row_tokens = tok_dev * n_head
    kv_dev = w_qkv.shape[1] // ((QPG + 2) * HD)
    row_index = lax.axis_index("tok")
    head_index = lax.axis_index("head")

    place_here = jnp.stack([row_index, head_index]).astype(jnp.int32)
    hidden, kv_cache, routes, place_here = lax.optimization_barrier(
        (hidden, kv_cache, routes, place_here)
    )
    states = spread(hidden, "head", bits_of(n_head))
    told = jnp.pad(
        routes.T.astype(jnp.bfloat16),
        ((0, TAIL - TOPK), (0, kv_cache.shape[1] - tok_dev)),
    )
    swap = min(2, n_tok // 2)
    walk = [bit for bit in bits_of(n_tok) if bit != swap]
    shards = spread(jnp.concatenate([kv_cache, told], axis=0), "tok", bits_of(n_tok))

    tied, _ = lax.optimization_barrier((place_here, shards[swap]))
    lead, rest = shares_of(tied, n_head, w_gate_up)
    lead = crossed(lead, "tok", swap)

    requests = jnp.stack([lengths, request_group]).astype(jnp.float32)
    requests = jnp.pad(requests, ((0, 6), (0, -requests.shape[1] % LANES)))
    half = HD // 2
    frequency = np.float32(ROPE_BASE) ** (-2.0 * np.arange(half, dtype=np.float32) / HD)
    frequency = np.tile(frequency.astype(np.float32), LANES // half)[None, :]
    n_pages = page_table.shape[0]
    pages = jnp.arange(n_pages, dtype=jnp.int32)
    place = jnp.sum(
        jnp.where(page_table[:, None] == pages[None, :], pages[:, None], 0), axis=0
    )
    columns = w_qkv.shape[1]
    queries, own_kv, column_table, row_table, in_first = pl.pallas_call(
        functools.partial(project_kernel, n_head, kv_dev),
        out_shape=[
            pltpu.VMEM((kv_dev, QPG, row_tokens, LANES), jnp.bfloat16),
            jax.ShapeDtypeStruct((row_tokens, kv_dev * LANES), jnp.bfloat16),
            pltpu.VMEM((row_tokens, LANES), jnp.float32),
            pltpu.VMEM((8, 2 * row_tokens), jnp.float32),
            jax.ShapeDtypeStruct((1,), jnp.int32),
        ],
        in_specs=[SMEM] + [VMEM] * (5 + n_head),
        out_specs=[VMEM] * 4 + [SMEM],
        compiler_params=params(32 if row_tokens <= 256 else 60),
        cost_estimate=spent(row_tokens * D * columns * 4),
        name="project",
    )(
        place_here,
        requests,
        key_mask.reshape(-1, tok_dev),
        frequency,
        attn_gain[None, :],
        pinned(jnp.pad(w_qkv, ((0, 0), (0, -columns % LANES)))),
        *[states[k] for k in range(n_head)],
    )
    prior_kv = lax.ppermute(own_kv, "tok", [(i, i + 1) for i in range(n_tok - 1)])
    pool_rows = kv_cache.shape[0] * n_tok
    rest, down, prior_kv = lax.optimization_barrier((rest, w_down, prior_kv))
    rest = crossed(rest, "tok", swap)
    down = crossed(down, "tok", swap)
    leads = spread(lead, "head", bits_of(n_head))
    queries, *leads = lax.optimization_barrier((queries, *[leads[k] for k in range(n_head)]))
    halves = [(0, kv_dev)]
    pieces = [[] for _ in range(n_head)]
    for heads_at in halves:
        count = heads_at[1]
        *contexts, all_routes = pl.pallas_call(
            functools.partial(attend_kernel, n_tok, heads_at, n_head),
            out_shape=[pltpu.VMEM((tok_dev, count * QPG * HD), jnp.bfloat16)] * n_head
            + [pltpu.VMEM((n_tok * TAIL, tok_dev), jnp.bfloat16)],
            in_specs=[SMEM] * 3 + [VMEM] * 5 + [pl.BlockSpec(memory_space=pltpu.HBM)] * n_tok,
            out_specs=[VMEM] * (n_head + 1),
            scratch_shapes=[pltpu.VMEM((pool_rows, count * LANES), jnp.bfloat16)]
            + [pltpu.VMEM((count, QPG, row_tokens, LANES), jnp.float32)] * 3
            + [pltpu.SemaphoreType.DMA] * 2,
            compiler_params=params(28),
            cost_estimate=spent(count * QPG * row_tokens * pool_rows * LANES * ATT),
            name="attend",
        )(
            place_here,
            in_first,
            place,
            queries,
            prior_kv,
            own_kv,
            column_table,
            row_table,
            *[shards[d] for d in range(n_tok)],
        )
        for k in range(n_head):
            pieces[k].append(crossed(contexts[k], "head", k) if k else contexts[0])
    rest, *ends = lax.optimization_barrier((rest, *[listed[0] for listed in pieces]))
    pieces = [[end] for end in ends]
    rests = spread(rest, "head", bits_of(n_head))
    attn_sum, mid_states, mixed = pl.pallas_call(
        functools.partial(close_kernel, n_head),
        out_shape=[jax.ShapeDtypeStruct(hidden.shape, jnp.bfloat16)] * 3,
        in_specs=[SMEM] + [VMEM] * (3 + n_head * len(halves)),
        out_specs=[VMEM] * 3,
        compiler_params=params(20),
        cost_estimate=spent(tok_dev * D * D * 4),
        name="close",
    )(
        place_here,
        hidden,
        pinned(o_weight),
        moe_gain[None, :],
        *[piece for listed in pieces for piece in listed],
    )

    slots, swapped = spread_by_stages(mixed, "tok", walk, [w[k] for k in range(n_head) for w in (leads, rests)] + [down])
    order = sorted(slots)
    w_gate_up, w_down, *swapped = [pinned(w) for w in (w_gate_up, w_down, *swapped)]
    parts = {}
    for first in range(0, len(order), 2):
        parts.update(
            run_experts(
                slots,
                order[first : first + 2],
                place_here,
                swap,
                all_routes,
                router.T,
                w_gate_up,
                w_down,
                swapped,
            )
        )
    routed_sum = folded(parts, "tok", walk[::-1]).astype(jnp.float32)
    layer_out = (mid_states.astype(jnp.float32) + routed_sum).astype(jnp.bfloat16)
    return (attn_sum, layer_out)


def solution(mesh):
    return jax.shard_map(
        per_device,
        mesh=mesh,
        in_specs=(
            P(("tok", "head"), None),
            P(),
            P(None, "head"),
            P("tok", "head"),
            P(),
            P(),
            P(),
            P(),
            P(),
            P(),
            P(),
            P(("tok", "head"), None),
            P("tok", None, None),
            P("tok", None, None),
        ),
        out_specs=(P(("tok", "head"), None), P(("tok", "head"), None)),
        check_vma=False,
    )
```

```python
import functools

import jax
import jax.numpy as jnp
import numpy as np
from jax import lax
from jax.experimental import pallas as pl
from jax.experimental.pallas import tpu as pltpu
from jax.sharding import PartitionSpec as P

D = 1536
HEADS = 24
KVH = 8
HD = 64
FFE = 512
TOPK = 8
PREFIX = 2048
GROUPS = 2
PAGE = 16
QPG = HEADS // KVH
BLOCK = 64


EPSILON = 1e-06
ROPE_BASE = 10000.0
MASKED = -1e30

LANES = 128


def crossed(array, axis, flip):
    count = lax.axis_size(axis)
    return lax.ppermute(array, axis, [(i, i ^ flip) for i in range(count)])


def spread(own, axis, bits):
    slots = {0: own}
    for bit in bits:
        for d in sorted(slots):
            slots[d | bit] = crossed(slots[d], axis, bit)
    return slots


def spread_by_stages(own, axis, bits, also):
    slots = {0: own}
    for stage in range(1, len(bits) + 1):
        coming = {}
        for d in slots:
            low = [bit for bit in bits if bit & d]
            for bit in bits[bits.index(low[-1]) + 1 if low else 0 :]:
                if bin(d).count("1") == stage - 1:
                    coming[d | bit] = crossed(slots[d], axis, bit)
        names = sorted(coming)
        came = lax.optimization_barrier([coming[d] for d in names] + (also if stage == 1 else []))
        slots.update(zip(names, came))
        also = came[len(names) :] if stage == 1 else also
    return slots, also


def folded(parts, axis, bits):
    parts = dict(parts)
    for bit in bits:
        for d in sorted(parts, reverse=True):
            if d & bit:
                came = crossed(parts.pop(d).astype(jnp.bfloat16), axis, bit)
                parts[d ^ bit] = parts[d ^ bit].astype(jnp.float32) + came.astype(jnp.float32)
    return parts[0]


def bits_of(count):
    return [1 << i for i in reversed(range(count.bit_length() - 1))]


VMEM = pl.BlockSpec(memory_space=pltpu.VMEM)
SMEM = pl.BlockSpec(memory_space=pltpu.SMEM)
TAIL = 16
ATT = 16


def params(mib):
    return pltpu.CompilerParams(vmem_limit_bytes=mib << 20)


def spent(flops):
    return pl.CostEstimate(flops=flops, transcendentals=0, bytes_accessed=0)


def pinned(array):
    return pltpu.with_memory_space_constraint(array, pltpu.VMEM)


def project_kernel(
    slots,
    kv_dev,
    where_ref,
    requests_ref,
    mask_ref,
    frequency_ref,
    gain_ref,
    weight_ref,
    *refs,
):
    state_refs = refs[:slots]
    query_ref, kv_ref, column_ref, row_ref, first_ref = refs[slots:]
    row_index, head_index = where_ref[0], where_ref[1]
    piece = state_refs[0].shape[0]
    rows = piece * slots
    real = jnp.float32
    rounded = jnp.bfloat16

    table = requests_ref[...]
    turned_table = jnp.transpose(table)
    width = table.shape[1]
    across = lax.broadcasted_iota(jnp.int32, (width, width), 1)
    along = lax.broadcasted_iota(jnp.int32, (width, width), 0)
    ends = jnp.sum(jnp.where(along <= across, turned_table[:, 0:1], 0.0), axis=0, keepdims=True)
    ends_up = jnp.sum(jnp.where(across <= along, table[0:1], 0.0), axis=1, keepdims=True)
    starts, starts_up = ends - table[0:1], ends_up - turned_table[:, 0:1]

    def offsets(shape, axis):
        place = lax.broadcasted_iota(jnp.int32, shape, axis)
        shift = jnp.zeros(shape, jnp.int32)
        for k in range(slots):
            shift = jnp.where(place // piece == k, ((head_index ^ k) - k) * piece, shift)
        return place + shift

    local, local_up = offsets((1, rows), 1), offsets((rows, 1), 0)
    across = lax.broadcasted_iota(jnp.int32, (rows, rows), 1).astype(real)
    along = lax.broadcasted_iota(jnp.int32, (rows, rows), 0).astype(real)
    lane = lax.broadcasted_iota(jnp.int32, (rows, LANES), 1)

    def tables(behind):
        first = (row_index - behind) * rows
        ids, ids_up = (local + first).astype(real), (local_up + first).astype(real)
        holds = (starts_up <= ids) & (ids < ends_up)
        holds_up = (starts <= ids_up) & (ids_up < ends)
        number = lax.broadcasted_iota(jnp.int32, (width, 1), 0).astype(real)
        request = jnp.sum(jnp.where(holds, number, 0.0), axis=0, keepdims=True)
        start = jnp.sum(jnp.where(holds, starts_up, 0.0), axis=0, keepdims=True)
        group = jnp.sum(jnp.where(holds, turned_table[:, 1:2], 0.0), axis=0, keepdims=True)
        group_up = jnp.sum(jnp.where(holds_up, table[1:2], 0.0), axis=1, keepdims=True)
        key = group * (2.0 * rows) + lax.broadcasted_iota(jnp.int32, (1, rows), 1).astype(real)
        key_up = group_up * (2.0 * rows) + lax.broadcasted_iota(jnp.int32, (rows, 1), 0).astype(real)
        rank = jnp.sum(jnp.where(key_up < key, 1.0, 0.0), axis=0, keepdims=True)
        rank_up = jnp.sum(jnp.where(key < key_up, 1.0, 0.0), axis=1, keepdims=True)
        place = rank == along

        def arranged(values):
            return jnp.sum(jnp.where(place, values, 0.0), axis=1, keepdims=True)

        marks = []
        for k in range(slots):
            block = (row_index - behind) * slots + (head_index ^ k)
            mark = mask_ref[pl.ds(jnp.maximum(block, 0), 1), :]
            marks.append(jnp.where(block >= 0, mark, 0))
        mark = jnp.concatenate(marks, axis=1)
        open_request = arranged(jnp.where(mark == 1, request, -1.0))
        ids = arranged(ids)
        columns = jnp.where(lane == 0, open_request, jnp.where(lane == 1, ids, 0.0))
        return columns, ids, arranged(request), arranged(start), place, rank_up, group

    before = tables(1)[0]
    columns, ids, request, start, place, rank_up, group = tables(0)
    columns = jnp.where(lane == 2, request, jnp.where(lane == 3, rank_up, columns))
    column_ref[...] = columns
    row_ref[:, :rows] = jnp.transpose(before)[:8]
    row_ref[:, rows:] = jnp.transpose(columns)[:8]
    first_ref[0] = jnp.sum(jnp.where(group == 0.0, 1.0, 0.0)).astype(jnp.int32)
    angles = (PREFIX + ids - start) * frequency_ref[...]
    cosine = jnp.cos(angles)
    sine = jnp.where(lane % HD < HD // 2, -1.0, 1.0) * jnp.sin(angles)

    states = jnp.concatenate([ref[...] for ref in state_refs], axis=0).astype(real)
    scale = lax.rsqrt(jnp.mean(states * states, axis=-1, keepdims=True) + EPSILON)
    normed = (states * scale * gain_ref[...]).astype(rounded)
    chosen = jnp.where(place, 1.0, 0.0).astype(rounded)
    normed = jnp.dot(chosen, normed, preferred_element_type=real).astype(rounded)
    projected = jnp.dot(normed, weight_ref[...], preferred_element_type=real)
    low = lane < HD
    first = lane % HD < HD // 2

    def tile(number):
        return projected[:, number * LANES : (number + 1) * LANES]

    @functools.cache
    def turned(number):
        plain = tile(number)
        partner = jnp.where(
            first, pltpu.roll(plain, LANES - HD // 2, 1), pltpu.roll(plain, HD // 2, 1)
        )
        return plain * cosine + partner * sine

    for j in range(kv_dev):
        unit = j * (QPG + 2)
        for i in range(QPG):
            query = turned((unit + i) // 2)
            if (unit + i) % 2:
                query = pltpu.roll(query, HD, 1)
            query_ref[j, i] = jnp.where(low, query * HD ** (-0.5), 0.0).astype(rounded)
        key, value = turned((unit + QPG) // 2), tile((unit + QPG + 1) // 2)
        if (unit + QPG) % 2:
            key, value = pltpu.roll(key, HD, 1), pltpu.roll(value, HD, 1)
        kv_ref[:, j * LANES : (j + 1) * LANES] = jnp.where(low, key, value).astype(rounded)


def scored(queries, keys):
    return lax.dot_general(
        queries, keys, (((1,), (1,)), ((), ())), preferred_element_type=jnp.float32
    )


def attend_kernel(
    shards,
    heads_at,
    slots,
    scalar_ref,
    first_ref,
    place_ref,
    query_ref,
    prior_ref,
    own_ref,
    column_ref,
    row_ref,
    *refs,
):
    shard_refs = refs[:shards]
    out_refs = refs[shards : shards + slots]
    routes_ref, stage_ref, pool_ref, peak_ref, total_ref, sum_ref, arrived = refs[shards + slots :]
    me = scalar_ref[0]
    in_first = first_ref[0]
    first_head, kv_dev = heads_at
    mine = slice(first_head * LANES, (first_head + kv_dev) * LANES)
    rows = query_ref.shape[2]
    blocks = rows // BLOCK
    shard_rows = shard_refs[0].shape[0] - TAIL
    shard_pages = shard_rows // PAGE

    for d in range(shards):
        pltpu.make_async_copy(shard_refs[d].at[:, mine], stage_ref.at[d], arrived).start()

    def near(b, carry):
        at = pl.ds(pl.multiple_of(b * BLOCK, BLOCK), BLOCK)
        column = column_ref[at, :]
        row = row_ref[...]
        allowed = (row[0:1] == column[:, 2:3]) & (row[1:2] <= column[:, 1:2])
        allowed = jnp.concatenate([allowed.astype(jnp.float32)] * QPG, axis=0) > 0.0
        for j in range(kv_dev):
            queries = query_ref[first_head + j, :, at, :].reshape(QPG * BLOCK, LANES)
            columns = slice((first_head + j) * LANES, (first_head + j + 1) * LANES)
            keys = jnp.concatenate([prior_ref[:, columns], own_ref[:, columns]], axis=0)
            scores = jnp.where(allowed, scored(queries, keys), MASKED)
            peak = jnp.max(scores, axis=-1, keepdims=True)
            weights = jnp.where(allowed, jnp.exp(scores - peak), 0.0)
            total = jnp.sum(weights, axis=-1, keepdims=True)
            mixed = jnp.dot(
                weights.astype(jnp.bfloat16), keys, preferred_element_type=jnp.float32
            )
            shape = (QPG, BLOCK, LANES)
            peak_ref[j, :, at, :] = jnp.broadcast_to(peak, mixed.shape).reshape(shape)
            total_ref[j, :, at, :] = jnp.broadcast_to(total, mixed.shape).reshape(shape)
            sum_ref[j, :, at, :] = mixed.reshape(shape)
        return carry

    lax.fori_loop(0, blocks, near, 0)
    pltpu.make_async_copy(stage_ref, stage_ref, arrived).wait()
    for d in range(shards):
        for j in range(shard_pages):
            at = pl.multiple_of(place_ref[(me ^ d) * shard_pages + j] * PAGE, PAGE)
            pool_ref[pl.ds(at, PAGE), :] = stage_ref[d, j * PAGE : (j + 1) * PAGE, :]
        routes_ref[d * TAIL : (d + 1) * TAIL, :] = stage_ref[
            d, shard_rows : shard_rows + TAIL, : routes_ref.shape[1]
        ]

    group_rows = pool_ref.shape[0] // GROUPS
    full = (in_first + BLOCK - 1) // BLOCK
    skip = in_first // BLOCK

    def far(item, carry):
        group = (item >= full).astype(jnp.int32)
        b = jnp.where(item < full, item, item - full + skip)
        at = pl.ds(pl.multiple_of(b * BLOCK, BLOCK), BLOCK)
        keys_at = pl.ds(pl.multiple_of(group * group_rows, group_rows), group_rows)
        line = lax.broadcasted_iota(jnp.int32, (QPG, BLOCK, LANES), 1) + b * BLOCK
        chosen = (line >= in_first) == (group == 1)
        shape = (QPG, BLOCK, LANES)
        for j in range(kv_dev):
            queries = query_ref[first_head + j, :, at, :].reshape(QPG * BLOCK, LANES)
            keys = pool_ref[keys_at, j * LANES : (j + 1) * LANES]
            scores = scored(queries, keys)
            here = jnp.max(scores, axis=-1, keepdims=True)
            weights = jnp.exp(scores - here)
            total = jnp.sum(weights, axis=-1, keepdims=True)
            mixed = jnp.dot(
                weights.astype(jnp.bfloat16), keys, preferred_element_type=jnp.float32
            ).reshape(shape)
            here = jnp.broadcast_to(here, (QPG * BLOCK, LANES)).reshape(shape)
            total = jnp.broadcast_to(total, (QPG * BLOCK, LANES)).reshape(shape)
            before = peak_ref[j, :, at, :]
            peak = jnp.maximum(before, here)
            keep, gain = jnp.exp(before - peak), jnp.exp(here - peak)
            joint_total = total_ref[j, :, at, :] * keep + total * gain
            joint_sum = sum_ref[j, :, at, :] * keep + mixed * gain
            total_ref[j, :, at, :] = jnp.where(chosen, joint_total, total_ref[j, :, at, :])
            sum_ref[j, :, at, :] = jnp.where(chosen, joint_sum, sum_ref[j, :, at, :])
        return carry

    lax.fori_loop(0, full + blocks - skip, far, 0)

    place = lax.broadcasted_iota(jnp.int32, (rows, rows), 1).astype(jnp.float32)
    back = jnp.where(column_ref[...][:, 3:4] == place, 1.0, 0.0).astype(jnp.bfloat16)
    lane = lax.broadcasted_iota(jnp.int32, (rows, LANES), 1)
    piece = rows // slots
    heads = [
        sum_ref[j, i] / total_ref[j, i] for j in range(kv_dev) for i in range(QPG)
    ]
    for h in range(0, len(heads), 2):
        pair = pltpu.roll(heads[h], HD, 1)
        if h + 1 < len(heads):
            pair = jnp.where(lane < HD, pair, heads[h + 1])
        pair = jnp.dot(
            back, pair.astype(jnp.bfloat16), preferred_element_type=jnp.float32
        ).astype(jnp.bfloat16)
        width = min(LANES, len(heads) * HD - h * HD)
        for k in range(slots):
            out_refs[k][:, h * HD : h * HD + width] = pair[k * piece : (k + 1) * piece, :width]


def close_kernel(slots, scalar_ref, hidden_ref, weight_ref, gain_ref, *refs):
    branch_ref, mid_ref, mixed_ref = refs[-3:]
    context_refs = refs[:-3]
    pieces = len(context_refs) // slots
    head_width = sum(ref.shape[1] for ref in context_refs[:pieces])
    total = None
    for k in range(slots):
        first = (scalar_ref[1] ^ k) * head_width
        for ref in context_refs[k * pieces : (k + 1) * pieces]:
            width = ref.shape[1]
            part = jnp.dot(
                ref[...],
                weight_ref[pl.ds(pl.multiple_of(first, HD), width), :],
                preferred_element_type=jnp.float32,
            )
            first = first + width
            total = part if total is None else total + part
    branch = total.astype(jnp.bfloat16)
    branch_ref[...] = branch
    mid = (hidden_ref[...].astype(jnp.float32) + branch.astype(jnp.float32)).astype(jnp.bfloat16)
    mid_ref[...] = mid
    wide = mid.astype(jnp.float32)
    scale = lax.rsqrt(jnp.mean(wide * wide, axis=-1, keepdims=True) + EPSILON)
    mixed_ref[...] = (wide * scale * gain_ref[...]).astype(jnp.bfloat16)


def expert_kernel(offsets, swap, parts, where_ref, *refs):
    count = len(offsets)
    state_refs = refs[:count]
    routes_ref, router_ref, up_ref, down_ref = refs[count : count + 4]
    swapped = refs[count + 4 : count + 4 + 2 * parts]
    other_ref = refs[count + 4 + 2 * parts]
    out_refs = refs[count + 5 + 2 * parts :]
    rows = state_refs[0].shape[0]
    lanes = router_ref.shape[0]
    experts_here = up_ref.shape[0]
    states = jnp.concatenate([ref[...] for ref in state_refs], axis=0)
    lane = lax.broadcasted_iota(jnp.int32, (rows, lanes), 1)
    hits = []
    for d in offsets:
        routes = routes_ref[d * TAIL : (d + 1) * TAIL, :].astype(jnp.float32)
        routes = jnp.transpose(routes).astype(jnp.int32)
        hit = jnp.zeros((rows, lanes), jnp.float32)
        for k in range(TOPK):
            hit = jnp.where(lane == routes[:, k : k + 1], 1.0, hit)
        hits.append(hit)
    hit = jnp.concatenate(hits, axis=0) > 0.0
    logits = scored(states, router_ref[...])
    logits = jnp.where(hit, logits, MASKED)
    peak = jnp.max(logits, axis=-1, keepdims=True)
    shares = jnp.where(hit, jnp.exp(logits - peak), 0.0)
    shares = shares / jnp.sum(shares, axis=-1, keepdims=True)
    lane = lax.broadcasted_iota(jnp.int32, shares.shape, 1)

    def gate_of(expert):
        return jnp.sum(jnp.where(lane == expert, shares, 0.0), axis=-1, keepdims=True)

    def through(lead, rest, down):
        activated = (lead / (1.0 + jnp.exp(-lead)) * rest).astype(jnp.bfloat16)
        return jnp.dot(activated, down, preferred_element_type=jnp.float32)

    result = None
    for x in range(experts_here):
        joined = jnp.dot(states, up_ref[x], preferred_element_type=jnp.float32)
        part = through(joined[:, :FFE], joined[:, FFE:], down_ref[x])
        part = gate_of(where_ref[0] * experts_here + x) * part
        result = part if result is None else result + part
    for x in range(experts_here):
        total = None
        for k in range(parts):
            lead_ref, rest_ref = swapped[2 * k : 2 * k + 2]
            share = lead_ref.shape[2]
            first = pl.multiple_of((where_ref[1] ^ k) * share, share)
            lead = jnp.dot(states, lead_ref[x], preferred_element_type=jnp.float32)
            rest = jnp.dot(states, rest_ref[x], preferred_element_type=jnp.float32)
            part = through(lead, rest, other_ref[x, pl.ds(first, share), :])
            total = part if total is None else total + part
        result = result + gate_of((where_ref[0] ^ swap) * experts_here + x) * total
    for i in range(count):
        out_refs[i][...] = result[i * rows : (i + 1) * rows].astype(jnp.bfloat16)


def run_experts(slots, offsets, where, swap, routes, router, w_gate_up, w_down, swapped):
    count = len(offsets)
    outs = pl.pallas_call(
        functools.partial(expert_kernel, offsets, swap, len(swapped) // 2),
        out_shape=[jax.ShapeDtypeStruct(slots[d].shape, jnp.bfloat16) for d in offsets],
        in_specs=[SMEM] + [VMEM] * (count + 4 + len(swapped)),
        out_specs=[VMEM] * count,
        compiler_params=params(28),
        cost_estimate=spent(count * 128 * D * FFE * 6 * 4),
        name="experts",
    )(where, *[slots[d] for d in offsets], routes, router, w_gate_up, w_down, *swapped)
    return dict(zip(offsets, outs))


def share_kernel(where_ref, up_ref, lead_ref, rest_ref, done):
    share = lead_ref.shape[2]
    at = pl.multiple_of(where_ref[1] * share, share)
    copies = [
        pltpu.make_async_copy(up_ref.at[:, :, pl.ds(at, share)], lead_ref, done.at[0]),
        pltpu.make_async_copy(up_ref.at[:, :, pl.ds(FFE + at, share)], rest_ref, done.at[1]),
    ]
    for copy in copies:
        copy.start()
    for copy in copies:
        copy.wait()


def shares_of(place_here, n_head, w_gate_up):
    share = FFE // n_head
    if share % LANES:
        first = place_here[1] * share
        return (
            lax.dynamic_slice_in_dim(w_gate_up, first, share, 2),
            lax.dynamic_slice_in_dim(w_gate_up, FFE + first, share, 2),
        )
    whole = pl.BlockSpec(memory_space=pltpu.HBM)
    return pl.pallas_call(
        share_kernel,
        out_shape=[pltpu.HBM((w_gate_up.shape[0], D, share), jnp.bfloat16)] * 2,
        in_specs=[SMEM, whole],
        out_specs=[whole] * 2,
        scratch_shapes=[pltpu.SemaphoreType.DMA((2,))],
        compiler_params=params(2),
        name="shares",
    )(place_here, w_gate_up)


def per_device(
    hidden,
    attn_gain,
    w_qkv,
    kv_cache,
    page_table,
    lengths,
    request_group,
    key_mask,
    o_weight,
    moe_gain,
    router,
    routes,
    w_gate_up,
    w_down,
):
    n_tok = lax.axis_size("tok")
    n_head = lax.axis_size("head")
    tok_dev = hidden.shape[0]
    row_tokens = tok_dev * n_head
    kv_dev = w_qkv.shape[1] // ((QPG + 2) * HD)
    row_index = lax.axis_index("tok")
    head_index = lax.axis_index("head")

    place_here = jnp.stack([row_index, head_index]).astype(jnp.int32)
    hidden, kv_cache, routes, place_here = lax.optimization_barrier(
        (hidden, kv_cache, routes, place_here)
    )
    states = spread(hidden, "head", bits_of(n_head))
    told = jnp.pad(
        routes.T.astype(jnp.bfloat16),
        ((0, TAIL - TOPK), (0, kv_cache.shape[1] - tok_dev)),
    )
    swap = min(2, n_tok // 2)
    walk = [bit for bit in bits_of(n_tok) if bit != swap]
    shards = spread(jnp.concatenate([kv_cache, told], axis=0), "tok", bits_of(n_tok))

    tied, _ = lax.optimization_barrier((place_here, shards[swap]))
    lead, rest = shares_of(tied, n_head, w_gate_up)
    lead = crossed(lead, "tok", swap)

    requests = jnp.stack([lengths, request_group]).astype(jnp.float32)
    requests = jnp.pad(requests, ((0, 6), (0, -requests.shape[1] % LANES)))
    half = HD // 2
    frequency = np.float32(ROPE_BASE) ** (-2.0 * np.arange(half, dtype=np.float32) / HD)
    frequency = np.tile(frequency.astype(np.float32), LANES // half)[None, :]
    n_pages = page_table.shape[0]
    pages = jnp.arange(n_pages, dtype=jnp.int32)
    place = jnp.sum(
        jnp.where(page_table[:, None] == pages[None, :], pages[:, None], 0), axis=0
    )
    columns = w_qkv.shape[1]
    queries, own_kv, column_table, row_table, in_first = pl.pallas_call(
        functools.partial(project_kernel, n_head, kv_dev),
        out_shape=[
            pltpu.VMEM((kv_dev, QPG, row_tokens, LANES), jnp.bfloat16),
            jax.ShapeDtypeStruct((row_tokens, kv_dev * LANES), jnp.bfloat16),
            pltpu.VMEM((row_tokens, LANES), jnp.float32),
            pltpu.VMEM((8, 2 * row_tokens), jnp.float32),
            jax.ShapeDtypeStruct((1,), jnp.int32),
        ],
        in_specs=[SMEM] + [VMEM] * (5 + n_head),
        out_specs=[VMEM] * 4 + [SMEM],
        compiler_params=params(32 if row_tokens <= 256 else 60),
        cost_estimate=spent(row_tokens * D * columns * 4),
        name="project",
    )(
        place_here,
        requests,
        key_mask.reshape(-1, tok_dev),
        frequency,
        attn_gain[None, :],
        pinned(jnp.pad(w_qkv, ((0, 0), (0, -columns % LANES)))),
        *[states[k] for k in range(n_head)],
    )
    prior_kv = lax.ppermute(own_kv, "tok", [(i, i + 1) for i in range(n_tok - 1)])
    pool_rows = kv_cache.shape[0] * n_tok
    rest, down, prior_kv = lax.optimization_barrier((rest, w_down, prior_kv))
    rest = crossed(rest, "tok", swap)
    down = crossed(down, "tok", swap)
    leads = spread(lead, "head", bits_of(n_head))
    queries, *leads = lax.optimization_barrier((queries, *[leads[k] for k in range(n_head)]))
    halves = [(0, kv_dev)]
    pieces = [[] for _ in range(n_head)]
    for heads_at in halves:
        count = heads_at[1]
        *contexts, all_routes = pl.pallas_call(
            functools.partial(attend_kernel, n_tok, heads_at, n_head),
            out_shape=[pltpu.VMEM((tok_dev, count * QPG * HD), jnp.bfloat16)] * n_head
            + [pltpu.VMEM((n_tok * TAIL, tok_dev), jnp.bfloat16)],
            in_specs=[SMEM] * 3 + [VMEM] * 5 + [pl.BlockSpec(memory_space=pltpu.HBM)] * n_tok,
            out_specs=[VMEM] * (n_head + 1),
            scratch_shapes=[
                pltpu.VMEM((n_tok, kv_cache.shape[0] + TAIL, count * LANES), jnp.bfloat16),
                pltpu.VMEM((pool_rows, count * LANES), jnp.bfloat16),
            ]
            + [pltpu.VMEM((count, QPG, row_tokens, LANES), jnp.float32)] * 3
            + [pltpu.SemaphoreType.DMA],
            compiler_params=params(34),
            cost_estimate=spent(count * QPG * row_tokens * pool_rows * LANES * ATT),
            name="attend",
        )(
            place_here,
            in_first,
            place,
            queries,
            prior_kv,
            own_kv,
            column_table,
            row_table,
            *[shards[d] for d in range(n_tok)],
        )
        for k in range(n_head):
            pieces[k].append(crossed(contexts[k], "head", k) if k else contexts[0])
    rest, *ends = lax.optimization_barrier((rest, *[listed[0] for listed in pieces]))
    pieces = [[end] for end in ends]
    rests = spread(rest, "head", bits_of(n_head))
    attn_sum, mid_states, mixed = pl.pallas_call(
        functools.partial(close_kernel, n_head),
        out_shape=[jax.ShapeDtypeStruct(hidden.shape, jnp.bfloat16)] * 3,
        in_specs=[SMEM] + [VMEM] * (3 + n_head * len(halves)),
        out_specs=[VMEM] * 3,
        compiler_params=params(20),
        cost_estimate=spent(tok_dev * D * D * 4),
        name="close",
    )(
        place_here,
        hidden,
        pinned(o_weight),
        moe_gain[None, :],
        *[piece for listed in pieces for piece in listed],
    )

    slots, swapped = spread_by_stages(mixed, "tok", walk, [w[k] for k in range(n_head) for w in (leads, rests)] + [down])
    order = sorted(slots)
    w_gate_up, w_down, *swapped = [pinned(w) for w in (w_gate_up, w_down, *swapped)]
    parts = {}
    for first in range(0, len(order), 2):
        parts.update(
            run_experts(
                slots,
                order[first : first + 2],
                place_here,
                swap,
                all_routes,
                router.T,
                w_gate_up,
                w_down,
                swapped,
            )
        )
    routed_sum = folded(parts, "tok", walk[::-1]).astype(jnp.float32)
    layer_out = (mid_states.astype(jnp.float32) + routed_sum).astype(jnp.bfloat16)
    return (attn_sum, layer_out)


def solution(mesh):
    return jax.shard_map(
        per_device,
        mesh=mesh,
        in_specs=(
            P(("tok", "head"), None),
            P(),
            P(None, "head"),
            P("tok", "head"),
            P(),
            P(),
            P(),
            P(),
            P(),
            P(),
            P(),
            P(("tok", "head"), None),
            P("tok", None, None),
            P("tok", None, None),
        ),
        out_specs=(P(("tok", "head"), None), P(("tok", "head"), None)),
        check_vma=False,
    )
```

```python
import functools

import jax
import jax.numpy as jnp
import numpy as np
from jax import lax
from jax.experimental import pallas as pl
from jax.experimental.pallas import tpu as pltpu
from jax.sharding import PartitionSpec as P

D = 1536
HEADS = 24
KVH = 8
HD = 64
FFE = 512
TOPK = 8
PREFIX = 2048
GROUPS = 2
PAGE = 16
QPG = HEADS // KVH
BLOCK = 64


EPSILON = 1e-06
ROPE_BASE = 10000.0
MASKED = -1e30

LANES = 128


def crossed(array, axis, flip):
    count = lax.axis_size(axis)
    return lax.ppermute(array, axis, [(i, i ^ flip) for i in range(count)])


def spread(own, axis, bits):
    slots = {0: own}
    for bit in bits:
        for d in sorted(slots):
            slots[d | bit] = crossed(slots[d], axis, bit)
    return slots


def spread_by_stages(own, axis, bits, also):
    slots = {0: own}
    for stage in range(1, len(bits) + 1):
        coming = {}
        for d in slots:
            low = [bit for bit in bits if bit & d]
            for bit in bits[bits.index(low[-1]) + 1 if low else 0 :]:
                if bin(d).count("1") == stage - 1:
                    coming[d | bit] = crossed(slots[d], axis, bit)
        names = sorted(coming)
        came = lax.optimization_barrier([coming[d] for d in names] + (also if stage == 1 else []))
        slots.update(zip(names, came))
        also = came[len(names) :] if stage == 1 else also
    return slots, also


def folded(parts, axis, bits):
    parts = dict(parts)
    for bit in bits:
        for d in sorted(parts, reverse=True):
            if d & bit:
                came = crossed(parts.pop(d).astype(jnp.bfloat16), axis, bit)
                parts[d ^ bit] = parts[d ^ bit].astype(jnp.float32) + came.astype(jnp.float32)
    return parts[0]


def bits_of(count):
    return [1 << i for i in reversed(range(count.bit_length() - 1))]


VMEM = pl.BlockSpec(memory_space=pltpu.VMEM)
SMEM = pl.BlockSpec(memory_space=pltpu.SMEM)
TAIL = 16
ATT = 16


def params(mib):
    return pltpu.CompilerParams(vmem_limit_bytes=mib << 20)


def spent(flops):
    return pl.CostEstimate(flops=flops, transcendentals=0, bytes_accessed=0)


def pinned(array):
    return pltpu.with_memory_space_constraint(array, pltpu.VMEM)


def project_kernel(
    slots,
    kv_dev,
    where_ref,
    requests_ref,
    mask_ref,
    frequency_ref,
    gain_ref,
    weight_ref,
    *refs,
):
    state_refs = refs[:slots]
    query_ref, kv_ref, column_ref, row_ref, first_ref = refs[slots:]
    row_index, head_index = where_ref[0], where_ref[1]
    piece = state_refs[0].shape[0]
    rows = piece * slots
    real = jnp.float32
    rounded = jnp.bfloat16

    table = requests_ref[...]
    turned_table = jnp.transpose(table)
    width = table.shape[1]
    across = lax.broadcasted_iota(jnp.int32, (width, width), 1)
    along = lax.broadcasted_iota(jnp.int32, (width, width), 0)
    ends = jnp.sum(jnp.where(along <= across, turned_table[:, 0:1], 0.0), axis=0, keepdims=True)
    ends_up = jnp.sum(jnp.where(across <= along, table[0:1], 0.0), axis=1, keepdims=True)
    starts, starts_up = ends - table[0:1], ends_up - turned_table[:, 0:1]

    def offsets(shape, axis):
        place = lax.broadcasted_iota(jnp.int32, shape, axis)
        shift = jnp.zeros(shape, jnp.int32)
        for k in range(slots):
            shift = jnp.where(place // piece == k, ((head_index ^ k) - k) * piece, shift)
        return place + shift

    local, local_up = offsets((1, rows), 1), offsets((rows, 1), 0)
    across = lax.broadcasted_iota(jnp.int32, (rows, rows), 1).astype(real)
    along = lax.broadcasted_iota(jnp.int32, (rows, rows), 0).astype(real)
    lane = lax.broadcasted_iota(jnp.int32, (rows, LANES), 1)

    def tables(behind):
        first = (row_index - behind) * rows
        ids, ids_up = (local + first).astype(real), (local_up + first).astype(real)
        holds = (starts_up <= ids) & (ids < ends_up)
        holds_up = (starts <= ids_up) & (ids_up < ends)
        number = lax.broadcasted_iota(jnp.int32, (width, 1), 0).astype(real)
        request = jnp.sum(jnp.where(holds, number, 0.0), axis=0, keepdims=True)
        start = jnp.sum(jnp.where(holds, starts_up, 0.0), axis=0, keepdims=True)
        group = jnp.sum(jnp.where(holds, turned_table[:, 1:2], 0.0), axis=0, keepdims=True)
        group_up = jnp.sum(jnp.where(holds_up, table[1:2], 0.0), axis=1, keepdims=True)
        key = group * (2.0 * rows) + lax.broadcasted_iota(jnp.int32, (1, rows), 1).astype(real)
        key_up = group_up * (2.0 * rows) + lax.broadcasted_iota(jnp.int32, (rows, 1), 0).astype(real)
        rank = jnp.sum(jnp.where(key_up < key, 1.0, 0.0), axis=0, keepdims=True)
        rank_up = jnp.sum(jnp.where(key < key_up, 1.0, 0.0), axis=1, keepdims=True)
        place = rank == along

        def arranged(values):
            return jnp.sum(jnp.where(place, values, 0.0), axis=1, keepdims=True)

        marks = []
        for k in range(slots):
            block = (row_index - behind) * slots + (head_index ^ k)
            mark = mask_ref[pl.ds(jnp.maximum(block, 0), 1), :]
            marks.append(jnp.where(block >= 0, mark, 0))
        mark = jnp.concatenate(marks, axis=1)
        open_request = arranged(jnp.where(mark == 1, request, -1.0))
        ids = arranged(ids)
        columns = jnp.where(lane == 0, open_request, jnp.where(lane == 1, ids, 0.0))
        return columns, ids, arranged(request), arranged(start), place, rank_up, group

    before = tables(1)[0]
    columns, ids, request, start, place, rank_up, group = tables(0)
    columns = jnp.where(lane == 2, request, jnp.where(lane == 3, rank_up, columns))
    column_ref[...] = columns
    row_ref[:, :rows] = jnp.transpose(before)[:8]
    row_ref[:, rows:] = jnp.transpose(columns)[:8]
    first_ref[0] = jnp.sum(jnp.where(group == 0.0, 1.0, 0.0)).astype(jnp.int32)
    angles = (PREFIX + ids - start) * frequency_ref[...]
    cosine = jnp.cos(angles)
    sine = jnp.where(lane % HD < HD // 2, -1.0, 1.0) * jnp.sin(angles)

    states = jnp.concatenate([ref[...] for ref in state_refs], axis=0).astype(real)
    scale = lax.rsqrt(jnp.mean(states * states, axis=-1, keepdims=True) + EPSILON)
    normed = (states * scale * gain_ref[...]).astype(rounded)
    chosen = jnp.where(place, 1.0, 0.0).astype(rounded)
    normed = jnp.dot(chosen, normed, preferred_element_type=real).astype(rounded)
    projected = jnp.dot(normed, weight_ref[...], preferred_element_type=real)
    low = lane < HD
    first = lane % HD < HD // 2

    def tile(number):
        return projected[:, number * LANES : (number + 1) * LANES]

    @functools.cache
    def turned(number):
        plain = tile(number)
        partner = jnp.where(
            first, pltpu.roll(plain, LANES - HD // 2, 1), pltpu.roll(plain, HD // 2, 1)
        )
        return plain * cosine + partner * sine

    for j in range(kv_dev):
        unit = j * (QPG + 2)
        for i in range(QPG):
            query = turned((unit + i) // 2)
            if (unit + i) % 2:
                query = pltpu.roll(query, HD, 1)
            query_ref[j, i] = jnp.where(low, query * HD ** (-0.5), 0.0).astype(rounded)
        key, value = turned((unit + QPG) // 2), tile((unit + QPG + 1) // 2)
        if (unit + QPG) % 2:
            key, value = pltpu.roll(key, HD, 1), pltpu.roll(value, HD, 1)
        kv_ref[:, j * LANES : (j + 1) * LANES] = jnp.where(low, key, value).astype(rounded)


def scored(queries, keys):
    return lax.dot_general(
        queries, keys, (((1,), (1,)), ((), ())), preferred_element_type=jnp.float32
    )


def attend_kernel(
    shards,
    heads_at,
    slots,
    scalar_ref,
    first_ref,
    place_ref,
    query_ref,
    prior_ref,
    own_ref,
    column_ref,
    row_ref,
    *refs,
):
    shard_refs = refs[:shards]
    out_refs = refs[shards : shards + slots]
    routes_ref, stage_ref, pool_ref, peak_ref, total_ref, sum_ref, arrived = refs[shards + slots :]
    me = scalar_ref[0]
    in_first = first_ref[0]
    first_head, kv_dev = heads_at
    mine = slice(first_head * LANES, (first_head + kv_dev) * LANES)
    rows = query_ref.shape[2]
    blocks = rows // BLOCK
    shard_rows = shard_refs[0].shape[0] - TAIL
    shard_pages = shard_rows // PAGE

    for d in range(shards):
        pltpu.make_async_copy(shard_refs[d].at[:, mine], stage_ref.at[d], arrived).start()

    def near(b, carry):
        at = pl.ds(pl.multiple_of(b * BLOCK, BLOCK), BLOCK)
        column = column_ref[at, :]
        row = row_ref[...]
        allowed = (row[0:1] == column[:, 2:3]) & (row[1:2] <= column[:, 1:2])
        allowed = jnp.concatenate([allowed.astype(jnp.float32)] * QPG, axis=0) > 0.0
        for j in range(kv_dev):
            queries = query_ref[first_head + j, :, at, :].reshape(QPG * BLOCK, LANES)
            columns = slice((first_head + j) * LANES, (first_head + j + 1) * LANES)
            keys = jnp.concatenate([prior_ref[:, columns], own_ref[:, columns]], axis=0)
            scores = jnp.where(allowed, scored(queries, keys), MASKED)
            peak = jnp.max(scores, axis=-1, keepdims=True)
            weights = jnp.where(allowed, jnp.exp(scores - peak), 0.0)
            total = jnp.sum(weights, axis=-1, keepdims=True)
            mixed = jnp.dot(
                weights.astype(jnp.bfloat16), keys, preferred_element_type=jnp.float32
            )
            shape = (QPG, BLOCK, LANES)
            peak_ref[j, :, at, :] = jnp.broadcast_to(peak, mixed.shape).reshape(shape)
            total_ref[j, :, at, :] = jnp.broadcast_to(total, mixed.shape).reshape(shape)
            sum_ref[j, :, at, :] = mixed.reshape(shape)
        return carry

    lax.fori_loop(0, blocks, near, 0)
    pltpu.make_async_copy(stage_ref, stage_ref, arrived).wait()
    for d in range(shards):
        for j in range(shard_pages):
            at = pl.multiple_of(place_ref[(me ^ d) * shard_pages + j] * PAGE, PAGE)
            pool_ref[pl.ds(at, PAGE), :] = stage_ref[d, j * PAGE : (j + 1) * PAGE, :]
        routes_ref[d * TAIL : (d + 1) * TAIL, :] = stage_ref[
            d, shard_rows : shard_rows + TAIL, : routes_ref.shape[1]
        ]

    group_rows = pool_ref.shape[0] // GROUPS
    full = (in_first + BLOCK - 1) // BLOCK
    skip = in_first // BLOCK

    def far(item, carry):
        group = (item >= full).astype(jnp.int32)
        b = jnp.where(item < full, item, item - full + skip)
        at = pl.ds(pl.multiple_of(b * BLOCK, BLOCK), BLOCK)
        keys_at = pl.ds(pl.multiple_of(group * group_rows, group_rows), group_rows)
        line = lax.broadcasted_iota(jnp.int32, (QPG, BLOCK, LANES), 1) + b * BLOCK
        chosen = (line >= in_first) == (group == 1)
        shape = (QPG, BLOCK, LANES)
        for j in range(kv_dev):
            queries = query_ref[first_head + j, :, at, :].reshape(QPG * BLOCK, LANES)
            keys = pool_ref[keys_at, j * LANES : (j + 1) * LANES]
            scores = scored(queries, keys)
            here = jnp.max(scores, axis=-1, keepdims=True)
            weights = jnp.exp(scores - here)
            total = jnp.sum(weights, axis=-1, keepdims=True)
            mixed = jnp.dot(
                weights.astype(jnp.bfloat16), keys, preferred_element_type=jnp.float32
            ).reshape(shape)
            here = jnp.broadcast_to(here, (QPG * BLOCK, LANES)).reshape(shape)
            total = jnp.broadcast_to(total, (QPG * BLOCK, LANES)).reshape(shape)
            before = peak_ref[j, :, at, :]
            peak = jnp.maximum(before, here)
            keep, gain = jnp.exp(before - peak), jnp.exp(here - peak)
            joint_total = total_ref[j, :, at, :] * keep + total * gain
            joint_sum = sum_ref[j, :, at, :] * keep + mixed * gain
            total_ref[j, :, at, :] = jnp.where(chosen, joint_total, total_ref[j, :, at, :])
            sum_ref[j, :, at, :] = jnp.where(chosen, joint_sum, sum_ref[j, :, at, :])
        return carry

    lax.fori_loop(0, full + blocks - skip, far, 0)

    place = lax.broadcasted_iota(jnp.int32, (rows, rows), 1).astype(jnp.float32)
    back = jnp.where(column_ref[...][:, 3:4] == place, 1.0, 0.0).astype(jnp.bfloat16)
    lane = lax.broadcasted_iota(jnp.int32, (rows, LANES), 1)
    piece = rows // slots
    heads = [
        sum_ref[j, i] / total_ref[j, i] for j in range(kv_dev) for i in range(QPG)
    ]
    for h in range(0, len(heads), 2):
        pair = pltpu.roll(heads[h], HD, 1)
        if h + 1 < len(heads):
            pair = jnp.where(lane < HD, pair, heads[h + 1])
        pair = jnp.dot(
            back, pair.astype(jnp.bfloat16), preferred_element_type=jnp.float32
        ).astype(jnp.bfloat16)
        width = min(LANES, len(heads) * HD - h * HD)
        for k in range(slots):
            out_refs[k][:, h * HD : h * HD + width] = pair[k * piece : (k + 1) * piece, :width]


def close_kernel(slots, scalar_ref, hidden_ref, weight_ref, gain_ref, *refs):
    branch_ref, mid_ref, mixed_ref = refs[-3:]
    context_refs = refs[:-3]
    pieces = len(context_refs) // slots
    head_width = sum(ref.shape[1] for ref in context_refs[:pieces])
    total = None
    for k in range(slots):
        first = (scalar_ref[1] ^ k) * head_width
        for ref in context_refs[k * pieces : (k + 1) * pieces]:
            width = ref.shape[1]
            part = jnp.dot(
                ref[...],
                weight_ref[pl.ds(pl.multiple_of(first, HD), width), :],
                preferred_element_type=jnp.float32,
            )
            first = first + width
            total = part if total is None else total + part
    branch = total.astype(jnp.bfloat16)
    branch_ref[...] = branch
    mid = (hidden_ref[...].astype(jnp.float32) + branch.astype(jnp.float32)).astype(jnp.bfloat16)
    mid_ref[...] = mid
    wide = mid.astype(jnp.float32)
    scale = lax.rsqrt(jnp.mean(wide * wide, axis=-1, keepdims=True) + EPSILON)
    mixed_ref[...] = (wide * scale * gain_ref[...]).astype(jnp.bfloat16)


def expert_kernel(offsets, swap, parts, where_ref, *refs):
    count = len(offsets)
    state_refs = refs[:count]
    routes_ref, router_ref, up_ref, down_ref = refs[count : count + 4]
    swapped = refs[count + 4 : count + 4 + 2 * parts]
    other_ref = refs[count + 4 + 2 * parts]
    out_refs = refs[count + 5 + 2 * parts :]
    rows = state_refs[0].shape[0]
    lanes = router_ref.shape[0]
    experts_here = up_ref.shape[0]
    states = jnp.concatenate([ref[...] for ref in state_refs], axis=0)
    lane = lax.broadcasted_iota(jnp.int32, (rows, lanes), 1)
    hits = []
    for d in offsets:
        routes = routes_ref[d * TAIL : (d + 1) * TAIL, :].astype(jnp.float32)
        routes = jnp.transpose(routes).astype(jnp.int32)
        hit = jnp.zeros((rows, lanes), jnp.float32)
        for k in range(TOPK):
            hit = jnp.where(lane == routes[:, k : k + 1], 1.0, hit)
        hits.append(hit)
    hit = jnp.concatenate(hits, axis=0) > 0.0
    logits = scored(states, router_ref[...])
    logits = jnp.where(hit, logits, MASKED)
    peak = jnp.max(logits, axis=-1, keepdims=True)
    shares = jnp.where(hit, jnp.exp(logits - peak), 0.0)
    shares = shares / jnp.sum(shares, axis=-1, keepdims=True)
    lane = lax.broadcasted_iota(jnp.int32, shares.shape, 1)

    def gate_of(expert):
        return jnp.sum(jnp.where(lane == expert, shares, 0.0), axis=-1, keepdims=True)

    def through(lead, rest, down):
        activated = (lead / (1.0 + jnp.exp(-lead)) * rest).astype(jnp.bfloat16)
        return jnp.dot(activated, down, preferred_element_type=jnp.float32)

    result = None
    for x in range(experts_here):
        joined = jnp.dot(states, up_ref[x], preferred_element_type=jnp.float32)
        part = through(joined[:, :FFE], joined[:, FFE:], down_ref[x])
        part = gate_of(where_ref[0] * experts_here + x) * part
        result = part if result is None else result + part
    for x in range(experts_here):
        total = None
        for k in range(parts):
            lead_ref, rest_ref = swapped[2 * k : 2 * k + 2]
            share = lead_ref.shape[2]
            first = pl.multiple_of((where_ref[1] ^ k) * share, share)
            lead = jnp.dot(states, lead_ref[x], preferred_element_type=jnp.float32)
            rest = jnp.dot(states, rest_ref[x], preferred_element_type=jnp.float32)
            part = through(lead, rest, other_ref[x, pl.ds(first, share), :])
            total = part if total is None else total + part
        result = result + gate_of((where_ref[0] ^ swap) * experts_here + x) * total
    for i in range(count):
        out_refs[i][...] = result[i * rows : (i + 1) * rows].astype(jnp.bfloat16)


def run_experts(slots, offsets, where, swap, routes, router, w_gate_up, w_down, swapped):
    count = len(offsets)
    outs = pl.pallas_call(
        functools.partial(expert_kernel, offsets, swap, len(swapped) // 2),
        out_shape=[jax.ShapeDtypeStruct(slots[d].shape, jnp.bfloat16) for d in offsets],
        in_specs=[SMEM] + [VMEM] * (count + 4 + len(swapped)),
        out_specs=[VMEM] * count,
        compiler_params=params(28),
        cost_estimate=spent(count * 128 * D * FFE * 6 * 4),
        name="experts",
    )(where, *[slots[d] for d in offsets], routes, router, w_gate_up, w_down, *swapped)
    return dict(zip(offsets, outs))


def share_kernel(where_ref, up_ref, lead_ref, rest_ref, done):
    share = lead_ref.shape[2]
    at = pl.multiple_of(where_ref[1] * share, share)
    copies = [
        pltpu.make_async_copy(up_ref.at[:, :, pl.ds(at, share)], lead_ref, done.at[0]),
        pltpu.make_async_copy(up_ref.at[:, :, pl.ds(FFE + at, share)], rest_ref, done.at[1]),
    ]
    for copy in copies:
        copy.start()
    for copy in copies:
        copy.wait()


def shares_of(place_here, n_head, w_gate_up):
    share = FFE // n_head
    if share % LANES:
        first = place_here[1] * share
        return (
            lax.dynamic_slice_in_dim(w_gate_up, first, share, 2),
            lax.dynamic_slice_in_dim(w_gate_up, FFE + first, share, 2),
        )
    whole = pl.BlockSpec(memory_space=pltpu.HBM)
    return pl.pallas_call(
        share_kernel,
        out_shape=[pltpu.HBM((w_gate_up.shape[0], D, share), jnp.bfloat16)] * 2,
        in_specs=[SMEM, whole],
        out_specs=[whole] * 2,
        scratch_shapes=[pltpu.SemaphoreType.DMA((2,))],
        compiler_params=params(2),
        name="shares",
    )(place_here, w_gate_up)


def per_device(
    hidden,
    attn_gain,
    w_qkv,
    kv_cache,
    page_table,
    lengths,
    request_group,
    key_mask,
    o_weight,
    moe_gain,
    router,
    routes,
    w_gate_up,
    w_down,
):
    n_tok = lax.axis_size("tok")
    n_head = lax.axis_size("head")
    tok_dev = hidden.shape[0]
    row_tokens = tok_dev * n_head
    kv_dev = w_qkv.shape[1] // ((QPG + 2) * HD)
    row_index = lax.axis_index("tok")
    head_index = lax.axis_index("head")

    place_here = jnp.stack([row_index, head_index]).astype(jnp.int32)
    hidden, kv_cache, routes, place_here = lax.optimization_barrier(
        (hidden, kv_cache, routes, place_here)
    )
    states = spread(hidden, "head", bits_of(n_head))
    told = jnp.pad(
        routes.T.astype(jnp.bfloat16),
        ((0, TAIL - TOPK), (0, kv_cache.shape[1] - tok_dev)),
    )
    swap = min(2, n_tok // 2)
    walk = [bit for bit in bits_of(n_tok) if bit != swap]
    shards = spread(jnp.concatenate([kv_cache, told], axis=0), "tok", bits_of(n_tok))

    tied, _ = lax.optimization_barrier((place_here, shards[1]))
    lead, rest = shares_of(tied, n_head, w_gate_up)
    lead = crossed(lead, "tok", swap)

    requests = jnp.stack([lengths, request_group]).astype(jnp.float32)
    requests = jnp.pad(requests, ((0, 6), (0, -requests.shape[1] % LANES)))
    half = HD // 2
    frequency = np.float32(ROPE_BASE) ** (-2.0 * np.arange(half, dtype=np.float32) / HD)
    frequency = np.tile(frequency.astype(np.float32), LANES // half)[None, :]
    n_pages = page_table.shape[0]
    pages = jnp.arange(n_pages, dtype=jnp.int32)
    place = jnp.sum(
        jnp.where(page_table[:, None] == pages[None, :], pages[:, None], 0), axis=0
    )
    columns = w_qkv.shape[1]
    queries, own_kv, column_table, row_table, in_first = pl.pallas_call(
        functools.partial(project_kernel, n_head, kv_dev),
        out_shape=[
            pltpu.VMEM((kv_dev, QPG, row_tokens, LANES), jnp.bfloat16),
            jax.ShapeDtypeStruct((row_tokens, kv_dev * LANES), jnp.bfloat16),
            pltpu.VMEM((row_tokens, LANES), jnp.float32),
            pltpu.VMEM((8, 2 * row_tokens), jnp.float32),
            jax.ShapeDtypeStruct((1,), jnp.int32),
        ],
        in_specs=[SMEM] + [VMEM] * (5 + n_head),
        out_specs=[VMEM] * 4 + [SMEM],
        compiler_params=params(32 if row_tokens <= 256 else 60),
        cost_estimate=spent(row_tokens * D * columns * 4),
        name="project",
    )(
        place_here,
        requests,
        key_mask.reshape(-1, tok_dev),
        frequency,
        attn_gain[None, :],
        pinned(jnp.pad(w_qkv, ((0, 0), (0, -columns % LANES)))),
        *[states[k] for k in range(n_head)],
    )
    prior_kv = lax.ppermute(own_kv, "tok", [(i, i + 1) for i in range(n_tok - 1)])
    pool_rows = kv_cache.shape[0] * n_tok
    rest, down, prior_kv = lax.optimization_barrier((rest, w_down, prior_kv))
    rest = crossed(rest, "tok", swap)
    down = crossed(down, "tok", swap)
    leads = spread(lead, "head", bits_of(n_head))
    queries, *leads = lax.optimization_barrier((queries, *[leads[k] for k in range(n_head)]))
    halves = [(0, kv_dev)]
    pieces = [[] for _ in range(n_head)]
    for heads_at in halves:
        count = heads_at[1]
        *contexts, all_routes = pl.pallas_call(
            functools.partial(attend_kernel, n_tok, heads_at, n_head),
            out_shape=[pltpu.VMEM((tok_dev, count * QPG * HD), jnp.bfloat16)] * n_head
            + [pltpu.VMEM((n_tok * TAIL, tok_dev), jnp.bfloat16)],
            in_specs=[SMEM] * 3 + [VMEM] * 5 + [pl.BlockSpec(memory_space=pltpu.HBM)] * n_tok,
            out_specs=[VMEM] * (n_head + 1),
            scratch_shapes=[
                pltpu.VMEM((n_tok, kv_cache.shape[0] + TAIL, count * LANES), jnp.bfloat16),
                pltpu.VMEM((pool_rows, count * LANES), jnp.bfloat16),
            ]
            + [pltpu.VMEM((count, QPG, row_tokens, LANES), jnp.float32)] * 3
            + [pltpu.SemaphoreType.DMA],
            compiler_params=params(34),
            cost_estimate=spent(count * QPG * row_tokens * pool_rows * LANES * ATT),
            name="attend",
        )(
            place_here,
            in_first,
            place,
            queries,
            prior_kv,
            own_kv,
            column_table,
            row_table,
            *[shards[d] for d in range(n_tok)],
        )
        for k in range(n_head):
            pieces[k].append(crossed(contexts[k], "head", k) if k else contexts[0])
    rest, *ends = lax.optimization_barrier((rest, *[listed[0] for listed in pieces]))
    pieces = [[end] for end in ends]
    rests = spread(rest, "head", bits_of(n_head))
    attn_sum, mid_states, mixed = pl.pallas_call(
        functools.partial(close_kernel, n_head),
        out_shape=[jax.ShapeDtypeStruct(hidden.shape, jnp.bfloat16)] * 3,
        in_specs=[SMEM] + [VMEM] * (3 + n_head * len(halves)),
        out_specs=[VMEM] * 3,
        compiler_params=params(20),
        cost_estimate=spent(tok_dev * D * D * 4),
        name="close",
    )(
        place_here,
        hidden,
        pinned(o_weight),
        moe_gain[None, :],
        *[piece for listed in pieces for piece in listed],
    )

    slots, swapped = spread_by_stages(mixed, "tok", walk, [w[k] for k in range(n_head) for w in (leads, rests)] + [down])
    order = sorted(slots)
    w_gate_up, w_down, *swapped = [pinned(w) for w in (w_gate_up, w_down, *swapped)]
    parts = {}
    for first in range(0, len(order), 2):
        parts.update(
            run_experts(
                slots,
                order[first : first + 2],
                place_here,
                swap,
                all_routes,
                router.T,
                w_gate_up,
                w_down,
                swapped,
            )
        )
    routed_sum = folded(parts, "tok", walk[::-1]).astype(jnp.float32)
    layer_out = (mid_states.astype(jnp.float32) + routed_sum).astype(jnp.bfloat16)
    return (attn_sum, layer_out)


def solution(mesh):
    return jax.shard_map(
        per_device,
        mesh=mesh,
        in_specs=(
            P(("tok", "head"), None),
            P(),
            P(None, "head"),
            P("tok", "head"),
            P(),
            P(),
            P(),
            P(),
            P(),
            P(),
            P(),
            P(("tok", "head"), None),
            P("tok", None, None),
            P("tok", None, None),
        ),
        out_specs=(P(("tok", "head"), None), P(("tok", "head"), None)),
        check_vma=False,
    )
```

```python
import functools

import jax
import jax.numpy as jnp
import numpy as np
from jax import lax
from jax.experimental import pallas as pl
from jax.experimental.pallas import tpu as pltpu
from jax.sharding import PartitionSpec as P

D = 1536
HEADS = 24
KVH = 8
HD = 64
FFE = 512
TOPK = 8
PREFIX = 2048
GROUPS = 2
PAGE = 16
QPG = HEADS // KVH
BLOCK = 64


EPSILON = 1e-06
ROPE_BASE = 10000.0
MASKED = -1e30

LANES = 128


def crossed(array, axis, flip):
    count = lax.axis_size(axis)
    return lax.ppermute(array, axis, [(i, i ^ flip) for i in range(count)])


def spread(own, axis, bits):
    slots = {0: own}
    for bit in bits:
        for d in sorted(slots):
            slots[d | bit] = crossed(slots[d], axis, bit)
    return slots


def spread_by_stages(own, axis, bits, also):
    slots = {0: own}
    for stage in range(1, len(bits) + 1):
        coming = {}
        for d in slots:
            low = [bit for bit in bits if bit & d]
            for bit in bits[bits.index(low[-1]) + 1 if low else 0 :]:
                if bin(d).count("1") == stage - 1:
                    coming[d | bit] = crossed(slots[d], axis, bit)
        names = sorted(coming)
        came = lax.optimization_barrier([coming[d] for d in names] + (also if stage == 1 else []))
        slots.update(zip(names, came))
        also = came[len(names) :] if stage == 1 else also
    return slots, also


def folded(parts, axis, bits):
    parts = dict(parts)
    for bit in bits:
        for d in sorted(parts, reverse=True):
            if d & bit:
                came = crossed(parts.pop(d).astype(jnp.bfloat16), axis, bit)
                parts[d ^ bit] = parts[d ^ bit].astype(jnp.float32) + came.astype(jnp.float32)
    return parts[0]


def bits_of(count):
    return [1 << i for i in reversed(range(count.bit_length() - 1))]


VMEM = pl.BlockSpec(memory_space=pltpu.VMEM)
SMEM = pl.BlockSpec(memory_space=pltpu.SMEM)
TAIL = 16
ATT = 16


def params(mib):
    return pltpu.CompilerParams(vmem_limit_bytes=mib << 20)


def spent(flops):
    return pl.CostEstimate(flops=flops, transcendentals=0, bytes_accessed=0)


def pinned(array):
    return pltpu.with_memory_space_constraint(array, pltpu.VMEM)


def project_kernel(
    slots,
    kv_dev,
    where_ref,
    requests_ref,
    mask_ref,
    frequency_ref,
    gain_ref,
    weight_ref,
    *refs,
):
    state_refs = refs[:slots]
    query_ref, kv_ref, column_ref, row_ref, first_ref = refs[slots:]
    row_index, head_index = where_ref[0], where_ref[1]
    piece = state_refs[0].shape[0]
    rows = piece * slots
    real = jnp.float32
    rounded = jnp.bfloat16

    table = requests_ref[...]
    turned_table = jnp.transpose(table)
    width = table.shape[1]
    across = lax.broadcasted_iota(jnp.int32, (width, width), 1)
    along = lax.broadcasted_iota(jnp.int32, (width, width), 0)
    ends = jnp.sum(jnp.where(along <= across, turned_table[:, 0:1], 0.0), axis=0, keepdims=True)
    ends_up = jnp.sum(jnp.where(across <= along, table[0:1], 0.0), axis=1, keepdims=True)
    starts, starts_up = ends - table[0:1], ends_up - turned_table[:, 0:1]

    def offsets(shape, axis):
        place = lax.broadcasted_iota(jnp.int32, shape, axis)
        shift = jnp.zeros(shape, jnp.int32)
        for k in range(slots):
            shift = jnp.where(place // piece == k, ((head_index ^ k) - k) * piece, shift)
        return place + shift

    local, local_up = offsets((1, rows), 1), offsets((rows, 1), 0)
    across = lax.broadcasted_iota(jnp.int32, (rows, rows), 1).astype(real)
    along = lax.broadcasted_iota(jnp.int32, (rows, rows), 0).astype(real)
    lane = lax.broadcasted_iota(jnp.int32, (rows, LANES), 1)

    def tables(behind):
        first = (row_index - behind) * rows
        ids, ids_up = (local + first).astype(real), (local_up + first).astype(real)
        holds = (starts_up <= ids) & (ids < ends_up)
        holds_up = (starts <= ids_up) & (ids_up < ends)
        number = lax.broadcasted_iota(jnp.int32, (width, 1), 0).astype(real)
        request = jnp.sum(jnp.where(holds, number, 0.0), axis=0, keepdims=True)
        start = jnp.sum(jnp.where(holds, starts_up, 0.0), axis=0, keepdims=True)
        group = jnp.sum(jnp.where(holds, turned_table[:, 1:2], 0.0), axis=0, keepdims=True)
        group_up = jnp.sum(jnp.where(holds_up, table[1:2], 0.0), axis=1, keepdims=True)
        key = group * (2.0 * rows) + lax.broadcasted_iota(jnp.int32, (1, rows), 1).astype(real)
        key_up = group_up * (2.0 * rows) + lax.broadcasted_iota(jnp.int32, (rows, 1), 0).astype(real)
        rank = jnp.sum(jnp.where(key_up < key, 1.0, 0.0), axis=0, keepdims=True)
        rank_up = jnp.sum(jnp.where(key < key_up, 1.0, 0.0), axis=1, keepdims=True)
        place = rank == along

        def arranged(values):
            return jnp.sum(jnp.where(place, values, 0.0), axis=1, keepdims=True)

        marks = []
        for k in range(slots):
            block = (row_index - behind) * slots + (head_index ^ k)
            mark = mask_ref[pl.ds(jnp.maximum(block, 0), 1), :]
            marks.append(jnp.where(block >= 0, mark, 0))
        mark = jnp.concatenate(marks, axis=1)
        open_request = arranged(jnp.where(mark == 1, request, -1.0))
        ids = arranged(ids)
        columns = jnp.where(lane == 0, open_request, jnp.where(lane == 1, ids, 0.0))
        return columns, ids, arranged(request), arranged(start), place, rank_up, group

    before = tables(1)[0]
    columns, ids, request, start, place, rank_up, group = tables(0)
    columns = jnp.where(lane == 2, request, jnp.where(lane == 3, rank_up, columns))
    column_ref[...] = columns
    row_ref[:, :rows] = jnp.transpose(before)[:8]
    row_ref[:, rows:] = jnp.transpose(columns)[:8]
    first_ref[0] = jnp.sum(jnp.where(group == 0.0, 1.0, 0.0)).astype(jnp.int32)
    angles = (PREFIX + ids - start) * frequency_ref[...]
    cosine = jnp.cos(angles)
    sine = jnp.where(lane % HD < HD // 2, -1.0, 1.0) * jnp.sin(angles)

    states = jnp.concatenate([ref[...] for ref in state_refs], axis=0).astype(real)
    scale = lax.rsqrt(jnp.mean(states * states, axis=-1, keepdims=True) + EPSILON)
    normed = (states * scale * gain_ref[...]).astype(rounded)
    chosen = jnp.where(place, 1.0, 0.0).astype(rounded)
    normed = jnp.dot(chosen, normed, preferred_element_type=real).astype(rounded)
    projected = jnp.dot(normed, weight_ref[...], preferred_element_type=real)
    low = lane < HD
    first = lane % HD < HD // 2

    def tile(number):
        return projected[:, number * LANES : (number + 1) * LANES]

    @functools.cache
    def turned(number):
        plain = tile(number)
        partner = jnp.where(
            first, pltpu.roll(plain, LANES - HD // 2, 1), pltpu.roll(plain, HD // 2, 1)
        )
        return plain * cosine + partner * sine

    for j in range(kv_dev):
        unit = j * (QPG + 2)
        for i in range(QPG):
            query = turned((unit + i) // 2)
            if (unit + i) % 2:
                query = pltpu.roll(query, HD, 1)
            query_ref[j, i] = jnp.where(low, query * HD ** (-0.5), 0.0).astype(rounded)
        key, value = turned((unit + QPG) // 2), tile((unit + QPG + 1) // 2)
        if (unit + QPG) % 2:
            key, value = pltpu.roll(key, HD, 1), pltpu.roll(value, HD, 1)
        kv_ref[:, j * LANES : (j + 1) * LANES] = jnp.where(low, key, value).astype(rounded)


def scored(queries, keys):
    return lax.dot_general(
        queries, keys, (((1,), (1,)), ((), ())), preferred_element_type=jnp.float32
    )


def attend_kernel(
    shards,
    heads_at,
    slots,
    scalar_ref,
    first_ref,
    place_ref,
    query_ref,
    prior_ref,
    own_ref,
    column_ref,
    row_ref,
    *refs,
):
    shard_refs = refs[:shards]
    out_refs = refs[shards : shards + slots]
    routes_ref, stage_ref, pool_ref, peak_ref, total_ref, sum_ref, arrived = refs[shards + slots :]
    me = scalar_ref[0]
    in_first = first_ref[0]
    first_head, kv_dev = heads_at
    mine = slice(first_head * LANES, (first_head + kv_dev) * LANES)
    rows = query_ref.shape[2]
    blocks = rows // BLOCK
    shard_rows = shard_refs[0].shape[0] - TAIL
    shard_pages = shard_rows // PAGE

    for d in range(shards):
        pltpu.make_async_copy(shard_refs[d].at[:, mine], stage_ref.at[d], arrived).start()

    def near(b, carry):
        at = pl.ds(pl.multiple_of(b * BLOCK, BLOCK), BLOCK)
        column = column_ref[at, :]
        row = row_ref[...]
        allowed = (row[0:1] == column[:, 2:3]) & (row[1:2] <= column[:, 1:2])
        allowed = jnp.concatenate([allowed.astype(jnp.float32)] * QPG, axis=0) > 0.0
        for j in range(kv_dev):
            queries = query_ref[first_head + j, :, at, :].reshape(QPG * BLOCK, LANES)
            columns = slice((first_head + j) * LANES, (first_head + j + 1) * LANES)
            keys = jnp.concatenate([prior_ref[:, columns], own_ref[:, columns]], axis=0)
            scores = jnp.where(allowed, scored(queries, keys), MASKED)
            peak = jnp.max(scores, axis=-1, keepdims=True)
            weights = jnp.exp(scores - peak)
            total = jnp.sum(weights, axis=-1, keepdims=True)
            mixed = jnp.dot(
                weights.astype(jnp.bfloat16), keys, preferred_element_type=jnp.float32
            )
            shape = (QPG, BLOCK, LANES)
            peak_ref[j, :, at, :] = jnp.broadcast_to(peak, mixed.shape).reshape(shape)
            total_ref[j, :, at, :] = jnp.broadcast_to(total, mixed.shape).reshape(shape)
            sum_ref[j, :, at, :] = mixed.reshape(shape)
        return carry

    lax.fori_loop(0, blocks, near, 0)
    pltpu.make_async_copy(stage_ref, stage_ref, arrived).wait()
    for d in range(shards):
        for j in range(shard_pages):
            at = pl.multiple_of(place_ref[(me ^ d) * shard_pages + j] * PAGE, PAGE)
            pool_ref[pl.ds(at, PAGE), :] = stage_ref[d, j * PAGE : (j + 1) * PAGE, :]
        routes_ref[d * TAIL : (d + 1) * TAIL, :] = stage_ref[
            d, shard_rows : shard_rows + TAIL, : routes_ref.shape[1]
        ]

    group_rows = pool_ref.shape[0] // GROUPS
    full = (in_first + BLOCK - 1) // BLOCK
    skip = in_first // BLOCK

    def far(item, carry):
        group = (item >= full).astype(jnp.int32)
        b = jnp.where(item < full, item, item - full + skip)
        at = pl.ds(pl.multiple_of(b * BLOCK, BLOCK), BLOCK)
        keys_at = pl.ds(pl.multiple_of(group * group_rows, group_rows), group_rows)
        line = lax.broadcasted_iota(jnp.int32, (QPG, BLOCK, LANES), 1) + b * BLOCK
        chosen = (line >= in_first) == (group == 1)
        shape = (QPG, BLOCK, LANES)
        for j in range(kv_dev):
            queries = query_ref[first_head + j, :, at, :].reshape(QPG * BLOCK, LANES)
            keys = pool_ref[keys_at, j * LANES : (j + 1) * LANES]
            scores = scored(queries, keys)
            here = jnp.max(scores, axis=-1, keepdims=True)
            weights = jnp.exp(scores - here)
            total = jnp.sum(weights, axis=-1, keepdims=True)
            mixed = jnp.dot(
                weights.astype(jnp.bfloat16), keys, preferred_element_type=jnp.float32
            ).reshape(shape)
            here = jnp.broadcast_to(here, (QPG * BLOCK, LANES)).reshape(shape)
            total = jnp.broadcast_to(total, (QPG * BLOCK, LANES)).reshape(shape)
            before = peak_ref[j, :, at, :]
            peak = jnp.maximum(before, here)
            keep, gain = jnp.exp(before - peak), jnp.exp(here - peak)
            joint_total = total_ref[j, :, at, :] * keep + total * gain
            joint_sum = sum_ref[j, :, at, :] * keep + mixed * gain
            total_ref[j, :, at, :] = jnp.where(chosen, joint_total, total_ref[j, :, at, :])
            sum_ref[j, :, at, :] = jnp.where(chosen, joint_sum, sum_ref[j, :, at, :])
        return carry

    lax.fori_loop(0, full + blocks - skip, far, 0)

    place = lax.broadcasted_iota(jnp.int32, (rows, rows), 1).astype(jnp.float32)
    back = jnp.where(column_ref[...][:, 3:4] == place, 1.0, 0.0).astype(jnp.bfloat16)
    lane = lax.broadcasted_iota(jnp.int32, (rows, LANES), 1)
    piece = rows // slots
    heads = [
        sum_ref[j, i] / total_ref[j, i] for j in range(kv_dev) for i in range(QPG)
    ]
    for h in range(0, len(heads), 2):
        pair = pltpu.roll(heads[h], HD, 1)
        if h + 1 < len(heads):
            pair = jnp.where(lane < HD, pair, heads[h + 1])
        pair = jnp.dot(
            back, pair.astype(jnp.bfloat16), preferred_element_type=jnp.float32
        ).astype(jnp.bfloat16)
        width = min(LANES, len(heads) * HD - h * HD)
        for k in range(slots):
            out_refs[k][:, h * HD : h * HD + width] = pair[k * piece : (k + 1) * piece, :width]


def close_kernel(slots, scalar_ref, hidden_ref, weight_ref, gain_ref, *refs):
    branch_ref, mid_ref, mixed_ref = refs[-3:]
    context_refs = refs[:-3]
    pieces = len(context_refs) // slots
    head_width = sum(ref.shape[1] for ref in context_refs[:pieces])
    total = None
    for k in range(slots):
        first = (scalar_ref[1] ^ k) * head_width
        for ref in context_refs[k * pieces : (k + 1) * pieces]:
            width = ref.shape[1]
            part = jnp.dot(
                ref[...],
                weight_ref[pl.ds(pl.multiple_of(first, HD), width), :],
                preferred_element_type=jnp.float32,
            )
            first = first + width
            total = part if total is None else total + part
    branch = total.astype(jnp.bfloat16)
    branch_ref[...] = branch
    mid = (hidden_ref[...].astype(jnp.float32) + branch.astype(jnp.float32)).astype(jnp.bfloat16)
    mid_ref[...] = mid
    wide = mid.astype(jnp.float32)
    scale = lax.rsqrt(jnp.mean(wide * wide, axis=-1, keepdims=True) + EPSILON)
    mixed_ref[...] = (wide * scale * gain_ref[...]).astype(jnp.bfloat16)


def expert_kernel(offsets, swap, parts, where_ref, *refs):
    count = len(offsets)
    state_refs = refs[:count]
    routes_ref, router_ref, up_ref, down_ref = refs[count : count + 4]
    swapped = refs[count + 4 : count + 4 + 2 * parts]
    other_ref = refs[count + 4 + 2 * parts]
    out_refs = refs[count + 5 + 2 * parts :]
    rows = state_refs[0].shape[0]
    lanes = router_ref.shape[0]
    experts_here = up_ref.shape[0]
    states = jnp.concatenate([ref[...] for ref in state_refs], axis=0)
    lane = lax.broadcasted_iota(jnp.int32, (rows, lanes), 1)
    hits = []
    for d in offsets:
        routes = routes_ref[d * TAIL : (d + 1) * TAIL, :].astype(jnp.float32)
        routes = jnp.transpose(routes).astype(jnp.int32)
        hit = jnp.zeros((rows, lanes), jnp.float32)
        for k in range(TOPK):
            hit = jnp.where(lane == routes[:, k : k + 1], 1.0, hit)
        hits.append(hit)
    hit = jnp.concatenate(hits, axis=0) > 0.0
    logits = scored(states, router_ref[...])
    logits = jnp.where(hit, logits, MASKED)
    peak = jnp.max(logits, axis=-1, keepdims=True)
    shares = jnp.where(hit, jnp.exp(logits - peak), 0.0)
    shares = shares / jnp.sum(shares, axis=-1, keepdims=True)
    lane = lax.broadcasted_iota(jnp.int32, shares.shape, 1)

    def gate_of(expert):
        return jnp.sum(jnp.where(lane == expert, shares, 0.0), axis=-1, keepdims=True)

    def through(lead, rest, down):
        activated = (lead / (1.0 + jnp.exp(-lead)) * rest).astype(jnp.bfloat16)
        return jnp.dot(activated, down, preferred_element_type=jnp.float32)

    result = None
    for x in range(experts_here):
        joined = jnp.dot(states, up_ref[x], preferred_element_type=jnp.float32)
        part = through(joined[:, :FFE], joined[:, FFE:], down_ref[x])
        part = gate_of(where_ref[0] * experts_here + x) * part
        result = part if result is None else result + part
    for x in range(experts_here):
        total = None
        for k in range(parts):
            lead_ref, rest_ref = swapped[2 * k : 2 * k + 2]
            share = lead_ref.shape[2]
            first = pl.multiple_of((where_ref[1] ^ k) * share, share)
            lead = jnp.dot(states, lead_ref[x], preferred_element_type=jnp.float32)
            rest = jnp.dot(states, rest_ref[x], preferred_element_type=jnp.float32)
            part = through(lead, rest, other_ref[x, pl.ds(first, share), :])
            total = part if total is None else total + part
        result = result + gate_of((where_ref[0] ^ swap) * experts_here + x) * total
    for i in range(count):
        out_refs[i][...] = result[i * rows : (i + 1) * rows].astype(jnp.bfloat16)


def run_experts(slots, offsets, where, swap, routes, router, w_gate_up, w_down, swapped):
    count = len(offsets)
    outs = pl.pallas_call(
        functools.partial(expert_kernel, offsets, swap, len(swapped) // 2),
        out_shape=[jax.ShapeDtypeStruct(slots[d].shape, jnp.bfloat16) for d in offsets],
        in_specs=[SMEM] + [VMEM] * (count + 4 + len(swapped)),
        out_specs=[VMEM] * count,
        compiler_params=params(28),
        cost_estimate=spent(count * 128 * D * FFE * 6 * 4),
        name="experts",
    )(where, *[slots[d] for d in offsets], routes, router, w_gate_up, w_down, *swapped)
    return dict(zip(offsets, outs))


def share_kernel(where_ref, up_ref, lead_ref, rest_ref, done):
    share = lead_ref.shape[2]
    at = pl.multiple_of(where_ref[1] * share, share)
    copies = [
        pltpu.make_async_copy(up_ref.at[:, :, pl.ds(at, share)], lead_ref, done.at[0]),
        pltpu.make_async_copy(up_ref.at[:, :, pl.ds(FFE + at, share)], rest_ref, done.at[1]),
    ]
    for copy in copies:
        copy.start()
    for copy in copies:
        copy.wait()


def shares_of(place_here, n_head, w_gate_up):
    share = FFE // n_head
    if share % LANES:
        first = place_here[1] * share
        return (
            lax.dynamic_slice_in_dim(w_gate_up, first, share, 2),
            lax.dynamic_slice_in_dim(w_gate_up, FFE + first, share, 2),
        )
    whole = pl.BlockSpec(memory_space=pltpu.HBM)
    return pl.pallas_call(
        share_kernel,
        out_shape=[pltpu.HBM((w_gate_up.shape[0], D, share), jnp.bfloat16)] * 2,
        in_specs=[SMEM, whole],
        out_specs=[whole] * 2,
        scratch_shapes=[pltpu.SemaphoreType.DMA((2,))],
        compiler_params=params(2),
        name="shares",
    )(place_here, w_gate_up)


def per_device(
    hidden,
    attn_gain,
    w_qkv,
    kv_cache,
    page_table,
    lengths,
    request_group,
    key_mask,
    o_weight,
    moe_gain,
    router,
    routes,
    w_gate_up,
    w_down,
):
    n_tok = lax.axis_size("tok")
    n_head = lax.axis_size("head")
    tok_dev = hidden.shape[0]
    row_tokens = tok_dev * n_head
    kv_dev = w_qkv.shape[1] // ((QPG + 2) * HD)
    row_index = lax.axis_index("tok")
    head_index = lax.axis_index("head")

    place_here = jnp.stack([row_index, head_index]).astype(jnp.int32)
    hidden, kv_cache, routes, place_here = lax.optimization_barrier(
        (hidden, kv_cache, routes, place_here)
    )
    states = spread(hidden, "head", bits_of(n_head))
    told = jnp.pad(
        routes.T.astype(jnp.bfloat16),
        ((0, TAIL - TOPK), (0, kv_cache.shape[1] - tok_dev)),
    )
    swap = min(2, n_tok // 2)
    walk = [bit for bit in bits_of(n_tok) if bit != swap]
    shards = spread(jnp.concatenate([kv_cache, told], axis=0), "tok", bits_of(n_tok))

    tied, _ = lax.optimization_barrier((place_here, shards[1]))
    lead, rest = shares_of(tied, n_head, w_gate_up)
    lead = crossed(lead, "tok", swap)

    requests = jnp.stack([lengths, request_group]).astype(jnp.float32)
    requests = jnp.pad(requests, ((0, 6), (0, -requests.shape[1] % LANES)))
    half = HD // 2
    frequency = np.float32(ROPE_BASE) ** (-2.0 * np.arange(half, dtype=np.float32) / HD)
    frequency = np.tile(frequency.astype(np.float32), LANES // half)[None, :]
    n_pages = page_table.shape[0]
    pages = jnp.arange(n_pages, dtype=jnp.int32)
    place = jnp.sum(
        jnp.where(page_table[:, None] == pages[None, :], pages[:, None], 0), axis=0
    )
    columns = w_qkv.shape[1]
    queries, own_kv, column_table, row_table, in_first = pl.pallas_call(
        functools.partial(project_kernel, n_head, kv_dev),
        out_shape=[
            pltpu.VMEM((kv_dev, QPG, row_tokens, LANES), jnp.bfloat16),
            jax.ShapeDtypeStruct((row_tokens, kv_dev * LANES), jnp.bfloat16),
            pltpu.VMEM((row_tokens, LANES), jnp.float32),
            pltpu.VMEM((8, 2 * row_tokens), jnp.float32),
            jax.ShapeDtypeStruct((1,), jnp.int32),
        ],
        in_specs=[SMEM] + [VMEM] * (5 + n_head),
        out_specs=[VMEM] * 4 + [SMEM],
        compiler_params=params(32 if row_tokens <= 256 else 60),
        cost_estimate=spent(row_tokens * D * columns * 4),
        name="project",
    )(
        place_here,
        requests,
        key_mask.reshape(-1, tok_dev),
        frequency,
        attn_gain[None, :],
        pinned(jnp.pad(w_qkv, ((0, 0), (0, -columns % LANES)))),
        *[states[k] for k in range(n_head)],
    )
    prior_kv = lax.ppermute(own_kv, "tok", [(i, i + 1) for i in range(n_tok - 1)])
    pool_rows = kv_cache.shape[0] * n_tok
    rest, down, prior_kv = lax.optimization_barrier((rest, w_down, prior_kv))
    rest = crossed(rest, "tok", swap)
    down = crossed(down, "tok", swap)
    leads = spread(lead, "head", bits_of(n_head))
    queries, *leads = lax.optimization_barrier((queries, *[leads[k] for k in range(n_head)]))
    halves = [(0, kv_dev)]
    pieces = [[] for _ in range(n_head)]
    for heads_at in halves:
        count = heads_at[1]
        *contexts, all_routes = pl.pallas_call(
            functools.partial(attend_kernel, n_tok, heads_at, n_head),
            out_shape=[pltpu.VMEM((tok_dev, count * QPG * HD), jnp.bfloat16)] * n_head
            + [pltpu.VMEM((n_tok * TAIL, tok_dev), jnp.bfloat16)],
            in_specs=[SMEM] * 3 + [VMEM] * 5 + [pl.BlockSpec(memory_space=pltpu.HBM)] * n_tok,
            out_specs=[VMEM] * (n_head + 1),
            scratch_shapes=[
                pltpu.VMEM((n_tok, kv_cache.shape[0] + TAIL, count * LANES), jnp.bfloat16),
                pltpu.VMEM((pool_rows, count * LANES), jnp.bfloat16),
            ]
            + [pltpu.VMEM((count, QPG, row_tokens, LANES), jnp.float32)] * 3
            + [pltpu.SemaphoreType.DMA],
            compiler_params=params(34),
            cost_estimate=spent(count * QPG * row_tokens * pool_rows * LANES * ATT),
            name="attend",
        )(
            place_here,
            in_first,
            place,
            queries,
            prior_kv,
            own_kv,
            column_table,
            row_table,
            *[shards[d] for d in range(n_tok)],
        )
        for k in range(n_head):
            pieces[k].append(crossed(contexts[k], "head", k) if k else contexts[0])
    rest, *ends = lax.optimization_barrier((rest, *[listed[0] for listed in pieces]))
    pieces = [[end] for end in ends]
    rests = spread(rest, "head", bits_of(n_head))
    attn_sum, mid_states, mixed = pl.pallas_call(
        functools.partial(close_kernel, n_head),
        out_shape=[jax.ShapeDtypeStruct(hidden.shape, jnp.bfloat16)] * 3,
        in_specs=[SMEM] + [VMEM] * (3 + n_head * len(halves)),
        out_specs=[VMEM] * 3,
        compiler_params=params(20),
        cost_estimate=spent(tok_dev * D * D * 4),
        name="close",
    )(
        place_here,
        hidden,
        pinned(o_weight),
        moe_gain[None, :],
        *[piece for listed in pieces for piece in listed],
    )

    slots, swapped = spread_by_stages(mixed, "tok", walk, [w[k] for k in range(n_head) for w in (leads, rests)] + [down])
    order = sorted(slots)
    w_gate_up, w_down, *swapped = [pinned(w) for w in (w_gate_up, w_down, *swapped)]
    parts = {}
    for first in range(0, len(order), 2):
        parts.update(
            run_experts(
                slots,
                order[first : first + 2],
                place_here,
                swap,
                all_routes,
                router.T,
                w_gate_up,
                w_down,
                swapped,
            )
        )
    routed_sum = folded(parts, "tok", walk[::-1]).astype(jnp.float32)
    layer_out = (mid_states.astype(jnp.float32) + routed_sum).astype(jnp.bfloat16)
    return (attn_sum, layer_out)


def solution(mesh):
    return jax.shard_map(
        per_device,
        mesh=mesh,
        in_specs=(
            P(("tok", "head"), None),
            P(),
            P(None, "head"),
            P("tok", "head"),
            P(),
            P(),
            P(),
            P(),
            P(),
            P(),
            P(),
            P(("tok", "head"), None),
            P("tok", None, None),
            P("tok", None, None),
        ),
        out_specs=(P(("tok", "head"), None), P(("tok", "head"), None)),
        check_vma=False,
    )
```
